256 devices in a mesh: region: 8 (over x, core), sub: 32 (over z, y).
Axes of the slice: x: 4, y: 4, z: 8, core: 2. Of those that a mesh axis runs over, the one named last changes fastest.
Arguments:
- observations: bfloat16 [262144, 256], P(('region', 'sub')), may hold values from -6 to 6
- basis_root: bfloat16 [262144, 512], P(('region', 'sub')), may hold values from -0.25 to 0.25
- basis_region: bfloat16 [262144, 512], P(('region', 'sub')), may hold values from -0.25 to 0.25
- noise_weights: float32 [262144], P(('region', 'sub')), may hold values from 0.3 to 4
- leaf_rows: int32 [256], P(('region', 'sub')), may hold values from 256 to 1024
- root_prior: float32 [512, 512], replicated, as said below
- region_prior: float32 [8, 512, 512], P('region'), as said below
Outputs:
- fitted: float32 [262144, 256], P(('region', 'sub'))
- root_mean: float32 [512, 256], replicated
The draws below stay inside these ranges and needn't reach their ends.
Inputs may be any that keep to these rules, and one draw needn't show every extreme that they name: `root_prior`: symmetric positive definite. `region_prior`: each symmetric positive definite.
All inputs are finite; a program needn't handle non-finite values.
Results may differ from the reference program's by a relative error of at most 0.0041.
Values sent between devices are 32-bit elements; how exact they have to be, the bound alone decides.
A program may use at most 64 MiB of HBM per device.

```python
import math
import jax
import jax.numpy as jnp
from jax import lax

K = 512
C = 256
CAP = 1024
REGIONS = 8
LEAVES = 256
ROWS = 262144
N_SUB = 32


def dominant(key):
    first, second = jax.random.split(key)
    diag = jax.random.uniform(first, (K,), jnp.float32, 2.0, 4.0)
    noise = 0.02 * jax.random.normal(second, (K, K), jnp.float32)
    return jnp.diag(diag) + noise + noise.T


def draw_root_prior(key, part):
    return dominant(jax.random.fold_in(key, 11))


def draw_region_prior(key, part):
    keys = jax.random.split(jax.random.fold_in(key, 23), REGIONS)
    return jax.vmap(dominant)(keys)


def place_ends(entries, own_key, smallest, largest):
    dims = entries.shape
    index_at = [jax.random.randint(jax.random.fold_in(own_key, axis), (), 0, dims[axis]) for axis in range(len(dims))]
    entries = entries.at[tuple(index_at)].set(smallest)
    longest = dims.index(max(dims))
    index_at[longest] = (index_at[longest] + 1) % dims[longest]
    return entries.at[tuple(index_at)].set(largest)


def level_of(rng, extent, cuts, least, top_value):
    level, own = 1.0, jax.random.fold_in(rng, 6)
    for position, blocks in cuts:
        heights = jnp.exp(jax.random.uniform(jax.random.fold_in(own, position), (blocks,), jnp.float32, least / len(cuts), top_value / len(cuts)))
        level = level * jnp.repeat(heights, extent[position] // blocks).reshape([-1 if axis == position else 1 for axis in range(len(extent))])
    return level


def normal_values(own_key, shape, deviation, limit, pieces=(), kind=jnp.bfloat16):
    gain = level_of(own_key, shape, pieces, -0.22, 0.18) if pieces else 1.0
    drawn = jax.random.normal(own_key, shape, jnp.float32) * deviation * gain
    return jnp.minimum(jnp.maximum(drawn, -limit), limit).astype(kind)


def setup_inputs(seed: int = 0) -> dict:
    splits = jax.random.split(jax.random.key(seed), 8)
    return {
        "observations": normal_values(splits[0], (ROWS, C), 1.0, 6.0, ((0, 256),)),
        "basis_root": normal_values(splits[1], (ROWS, K), K ** -0.5, 0.25, ((0, 256),)),
        "basis_region": normal_values(splits[2], (ROWS, K), K ** -0.5, 0.25, ((0, 256),)),
        "noise_weights": jnp.clip(jnp.exp(math.log(4.0) - 2.5902671 * jax.random.uniform(splits[3], (ROWS,), jnp.float32) ** level_of(splits[3], (ROWS,), ((0, 256),), -0.2, 0.2)), 0.3, 4.0),
        "leaf_rows": place_ends(jax.random.randint(splits[4], (LEAVES,), CAP // 4, CAP + 1), jax.random.fold_in(splits[4], 1), CAP // 4, CAP).astype(jnp.int32),
        "root_prior": draw_root_prior(jax.random.fold_in(splits[7], 71), 0),
        "region_prior": draw_region_prior(jax.random.fold_in(splits[7], 71), 0),
    }


def gram(left, right):
    return lax.dot_general(left.astype(jnp.float32), right.astype(jnp.float32), (((0,), (0,)), ((), ())), preferred_element_type=jnp.float32)

def hdot(a, b):
    return jnp.dot(a, b, precision=lax.Precision.HIGHEST)

def region_section(items):
    obs, broot, bregion, weights, counts, prior = items
    slots = jnp.arange(CAP, dtype=jnp.int32)

    def leaf(carry, parts):
        o, b0, b1, w, n = parts
        weight = jnp.where(slots < n, w, jnp.zeros_like(w))
        w0 = (b0 * weight[:, None]).astype(jnp.bfloat16)
        w1 = (b1 * weight[:, None]).astype(jnp.bfloat16)
        terms = (gram(w0, b0), gram(w0, b1), gram(w1, b1), gram(w0, o), gram(w1, o))
        return (tuple((c + t for c, t in zip(carry, terms))), None)
    zero_kk = jnp.zeros((K, K), jnp.float32)
    zero_kc = jnp.zeros((K, C), jnp.float32)
    init = (zero_kk, zero_kk, zero_kk, zero_kc, zero_kc)
    sums, unused = lax.scan(leaf, init, (obs, broot, bregion, weights, counts))
    a00, a01, a11, w0, w1 = sums
    factor = jnp.linalg.cholesky(prior + a11)
    solved = jax.scipy.linalg.cho_solve((factor, True), jnp.concatenate([a01.T, w1], axis=1))
    schur = a00 - hdot(a01, solved[:, :K])
    tail = w0 - hdot(a01, solved[:, K:])
    return (schur, tail, solved)

def reference(observations, basis_root, basis_region, noise_weights, leaf_rows, root_prior, region_prior):
    obs = observations.reshape(REGIONS, N_SUB, CAP, C)
    broot = basis_root.reshape(REGIONS, N_SUB, CAP, K)
    bregion = basis_region.reshape(REGIONS, N_SUB, CAP, K)
    weights = noise_weights.reshape(REGIONS, N_SUB, CAP)
    counts = leaf_rows.reshape(REGIONS, N_SUB)
    schur, tail, solved = lax.map(region_section, (obs, broot, bregion, weights, counts, region_prior))
    factor = jnp.linalg.cholesky(root_prior + jnp.sum(schur, axis=0))
    root_mean = jax.scipy.linalg.cho_solve((factor, True), jnp.sum(tail, axis=0))
    root_low = root_mean.astype(jnp.bfloat16)

    def predict(items):
        b0, b1, sol = items
        region_low = (sol[:, K:] - hdot(sol[:, :K], root_mean)).astype(jnp.bfloat16)
        flat0 = b0.reshape(N_SUB * CAP, K)
        flat1 = b1.reshape(N_SUB * CAP, K)
        return jnp.dot(flat0.astype(jnp.float32), root_low.astype(jnp.float32), preferred_element_type=jnp.float32) + jnp.dot(flat1.astype(jnp.float32), region_low.astype(jnp.float32), preferred_element_type=jnp.float32)
    fitted = lax.map(predict, (broot, bregion, solved)).reshape(ROWS, C)
    return (fitted, root_mean)
```

```python
import jax
import jax.numpy as jnp
from jax import lax
from jax.experimental import pallas as pl
from jax.experimental.pallas import tpu as pltpu
from jax.sharding import PartitionSpec as P

F32 = jnp.float32
BF16 = jnp.bfloat16
HI = lax.Precision.HIGHEST

def split(x):
    hi = x.astype(BF16)
    return hi, (x - hi.astype(F32)).astype(BF16)

def dot3(a, b, dims):
    ah, al = a
    bh, bl = b
    d = lambda u, v: lax.dot_general(u, v, (dims, ((), ())), preferred_element_type=F32)
    return d(ah, bh) + (d(ah, bl) + d(al, bh))

MM = ((1,), (0,))

def inv_small(s):
    s = dict(s)
    g = lambda i, j: s[(i, j)] if i >= j else s[(j, i)]
    for k in range(0, 8, 2):
        a, b, c = g(k, k), g(k + 1, k), g(k + 1, k + 1)
        r = 1.0 / (a * c - b * b)
        d00, d01, d11 = c * r, -b * r, a * r
        others = [i for i in range(8) if i not in (k, k + 1)]
        t = {}
        for i in others:
            u, v = g(i, k), g(i, k + 1)
            t[i] = (u * d00 + v * d01, u * d01 + v * d11)
        new = {}
        for i in others:
            for j in others:
                if i >= j:
                    new[(i, j)] = g(i, j) - (t[i][0] * g(j, k) + t[i][1] * g(j, k + 1))
        for i in others:
            for q in (0, 1):
                key = (max(i, k + q), min(i, k + q))
                new[key] = t[i][q]
        new[(k, k)], new[(k + 1, k)], new[(k + 1, k + 1)] = -d00, -d01, -d11
        s = new
    return {key: -v for key, v in s.items()}

def inv128(rows):
    lane = lax.broadcasted_iota(jnp.int32, (8, 128), 1)
    sub = lax.broadcasted_iota(jnp.int32, (8, 128), 0)
    a = list(rows)
    for p in range(16):
        R = a[p]
        k0 = 8 * p
        inK = (lane >= k0) & (lane < k0 + 8)
        cols = [jnp.broadcast_to(R[:, k0 + j:k0 + j + 1], (8, 128)) for j in range(8)]
        s = {(i, j): jnp.broadcast_to(cols[j][i:i + 1, :], (8, 128)) for i in range(8) for j in range(i + 1)}
        Rm = jnp.where(inK, jnp.where(lane - k0 == sub, -1.0, 0.0), R)
        Rb = [jnp.broadcast_to(Rm[q:q + 1, :], (8, 128)) for q in range(8)]
        D = inv_small(s)
        g = lambda i, j: D[(i, j)] if i >= j else D[(j, i)]
        G = []
        for i in range(8):
            t = [g(i, q) * Rb[q] for q in range(8)]
            while len(t) > 1:
                t = [t[m] + t[m + 1] for m in range(0, len(t), 2)]
            G.append(t[0])
        order = [i % 16 for i in range(p + 1, p + 16)]
        for i in order:
            c = [jnp.broadcast_to(a[i][:, k0 + j:k0 + j + 1], (8, 128)) * G[j] for j in range(8)]
            while len(c) > 1:
                c = [c[m] + c[m + 1] for m in range(0, len(c), 2)]
            a[i] = jnp.where(inK, 0.0, a[i]) - c[0]
        new = G[7]
        for q in range(7):
            new = jnp.where(sub == q, G[q], new)
        a[p] = new
    return a

def spd_inverse(A, Dbuf, n=512):
    nb = n // 128
    def step(k, carry):
        o = pl.multiple_of(k * 128, 128)
        rows = [A[pl.ds(pl.multiple_of(o + 8 * i, 8), 8), pl.ds(o, 128)] for i in range(16)]
        out = inv128(rows)
        for i in range(16):
            Dbuf[8 * i:8 * i + 8, :] = -out[i]
        D = split(Dbuf[...])
        Rk = split(A[pl.ds(o, 128), :])
        Ck = split(A[:, pl.ds(o, 128)])
        G = dot3(D, Rk, MM)
        T = dot3(Ck, D, MM)
        U = dot3(Ck, split(G), MM)
        A[...] = A[...] - U
        A[pl.ds(o, 128), :] = G
        A[:, pl.ds(o, 128)] = T
        A[pl.ds(o, 128), pl.ds(o, 128)] = -Dbuf[...]
        return carry
    lax.fori_loop(0, nb, step, 0)

def inverse_kernel(x_ref, o_ref, A, D):
    A[...] = x_ref[...]
    spd_inverse(A, D)
    o_ref[...] = -A[...]

def inverse(x):
    return pl.pallas_call(inverse_kernel, out_shape=jax.ShapeDtypeStruct(x.shape, F32),
        in_specs=[pl.BlockSpec(memory_space=pltpu.VMEM)], out_specs=pl.BlockSpec(memory_space=pltpu.VMEM),
        scratch_shapes=[pltpu.VMEM((512, 512), F32), pltpu.VMEM((128, 128), F32)])(x)


def gram(left, right):
    return lax.dot_general(
        left, right, (((0,), (0,)), ((), ())), preferred_element_type=jnp.float32
    )


def hdot(a, b):
    return jnp.dot(a, b, precision=lax.Precision.HIGHEST)


def body(
    observations, basis_root, basis_region, noise_weights, leaf_rows, root_prior, region_prior
):
    slots = observations.shape[0]
    knots = basis_root.shape[1]
    live = jnp.arange(slots, dtype=jnp.int32) < leaf_rows[0]
    weight = jnp.where(live, noise_weights, jnp.zeros_like(noise_weights))
    weighted_root = (basis_root * weight[:, None]).astype(jnp.bfloat16)
    weighted_region = (basis_region * weight[:, None]).astype(jnp.bfloat16)
    g00 = gram(weighted_root, basis_root)
    g01 = gram(weighted_root, basis_region)
    g11 = gram(weighted_region, basis_region)
    o0 = gram(weighted_root, observations)
    o1 = gram(weighted_region, observations)
    a00, a01, a11, w0, w1 = lax.psum((g00, g01, g11, o0, o1), "sub")
    system = region_prior[0] + a11
    region_inverse = inverse((system + system.T) * 0.5)
    solved = hdot(region_inverse, jnp.concatenate([a01.T, w1], axis=1))
    schur = a00 - hdot(a01, solved[:, :knots])
    tail = w0 - hdot(a01, solved[:, knots:])
    schur_total, tail_total = lax.psum((schur, tail), "region")
    root = root_prior + schur_total
    root_mean = hdot(inverse((root + root.T) * 0.5), tail_total)
    region_mean = solved[:, knots:] - hdot(solved[:, :knots], root_mean)
    fitted = jnp.dot(basis_root, root_mean.astype(jnp.bfloat16), preferred_element_type=jnp.float32)
    fitted = fitted + jnp.dot(
        basis_region, region_mean.astype(jnp.bfloat16), preferred_element_type=jnp.float32
    )
    return (fitted, root_mean)


def solution(mesh):
    placed = (
        P(("region", "sub"), None),
        P(("region", "sub"), None),
        P(("region", "sub"), None),
        P(("region", "sub")),
        P(("region", "sub")),
        P(),
        P("region", None, None),
    )
    return jax.shard_map(
        body,
        mesh=mesh,
        in_specs=placed,
        out_specs=(P(("region", "sub"), None), P()),
        check_vma=False,
    )
```

```python
import functools

import jax
import jax.numpy as jnp
from jax import lax
from jax.experimental import pallas as pl
from jax.experimental.pallas import tpu as pltpu
from jax.sharding import PartitionSpec as P

MESH = pl.DeviceIdType.MESH
F32 = jnp.float32
BF16 = jnp.bfloat16
HI = lax.Precision.HIGHEST

def split(x):
    hi = x.astype(BF16)
    return hi, (x - hi.astype(F32)).astype(BF16)

def dot3(a, b, dims):
    ah, al = a
    bh, bl = b
    d = lambda u, v: lax.dot_general(u, v, (dims, ((), ())), preferred_element_type=F32)
    return d(ah, bh) + (d(ah, bl) + d(al, bh))

MM = ((1,), (0,))

def inv_small(s):
    s = dict(s)
    g = lambda i, j: s[(i, j)] if i >= j else s[(j, i)]
    for k in range(0, 8, 2):
        a, b, c = g(k, k), g(k + 1, k), g(k + 1, k + 1)
        r = 1.0 / (a * c - b * b)
        d00, d01, d11 = c * r, -b * r, a * r
        others = [i for i in range(8) if i not in (k, k + 1)]
        t = {}
        for i in others:
            u, v = g(i, k), g(i, k + 1)
            t[i] = (u * d00 + v * d01, u * d01 + v * d11)
        new = {}
        for i in others:
            for j in others:
                if i >= j:
                    new[(i, j)] = g(i, j) - (t[i][0] * g(j, k) + t[i][1] * g(j, k + 1))
        for i in others:
            for q in (0, 1):
                key = (max(i, k + q), min(i, k + q))
                new[key] = t[i][q]
        new[(k, k)], new[(k + 1, k)], new[(k + 1, k + 1)] = -d00, -d01, -d11
        s = new
    return {key: -v for key, v in s.items()}

def inv128(rows):
    lane = lax.broadcasted_iota(jnp.int32, (8, 128), 1)
    sub = lax.broadcasted_iota(jnp.int32, (8, 128), 0)
    a = list(rows)
    for p in range(16):
        R = a[p]
        k0 = 8 * p
        inK = (lane >= k0) & (lane < k0 + 8)
        cols = [jnp.broadcast_to(R[:, k0 + j:k0 + j + 1], (8, 128)) for j in range(8)]
        s = {(i, j): jnp.broadcast_to(cols[j][i:i + 1, :], (8, 128)) for i in range(8) for j in range(i + 1)}
        Rm = jnp.where(inK, jnp.where(lane - k0 == sub, -1.0, 0.0), R)
        Rb = [jnp.broadcast_to(Rm[q:q + 1, :], (8, 128)) for q in range(8)]
        D = inv_small(s)
        g = lambda i, j: D[(i, j)] if i >= j else D[(j, i)]
        G = []
        for i in range(8):
            t = [g(i, q) * Rb[q] for q in range(8)]
            while len(t) > 1:
                t = [t[m] + t[m + 1] for m in range(0, len(t), 2)]
            G.append(t[0])
        order = [i % 16 for i in range(p + 1, p + 16)]
        for i in order:
            c = [jnp.broadcast_to(a[i][:, k0 + j:k0 + j + 1], (8, 128)) * G[j] for j in range(8)]
            while len(c) > 1:
                c = [c[m] + c[m + 1] for m in range(0, len(c), 2)]
            a[i] = jnp.where(inK, 0.0, a[i]) - c[0]
        new = G[7]
        for q in range(7):
            new = jnp.where(sub == q, G[q], new)
        a[p] = new
    return a

def spd_inverse(A, Dbuf, n=512, serve=None):
    nb = n // 128
    def step(k, carry):
        o = k * 128 if serve is not None else pl.multiple_of(k * 128, 128)
        rows = [A[pl.ds(o + 8 * i if serve is not None else pl.multiple_of(o + 8 * i, 8), 8), pl.ds(o, 128)] for i in range(16)]
        out = inv128(rows)
        for i in range(16):
            Dbuf[8 * i:8 * i + 8, :] = -out[i]
        D = split(Dbuf[...])
        Rk = split(A[pl.ds(o, 128), :])
        Ck = split(A[:, pl.ds(o, 128)])
        G = dot3(D, Rk, MM)
        T = dot3(Ck, D, MM)
        U = dot3(Ck, split(G), MM)
        A[...] = A[...] - U
        A[pl.ds(o, 128), :] = G
        A[:, pl.ds(o, 128)] = T
        A[pl.ds(o, 128), pl.ds(o, 128)] = -Dbuf[...]
        return carry
    if serve is None:
        lax.fori_loop(0, nb, step, 0)
    else:
        for k in range(nb):
            step(k, 0)
            serve(k)


NT = ((1,), (1,))
TN = ((0,), (0,))


class Copies:
    def __init__(self, send_sems, recv_sems):
        self.send_sems, self.recv_sems, self.used, self.sent = send_sems, recv_sems, 0, []

    def slots(self, count):
        first = self.used
        self.used += count
        return first

    def start(self, source, target, slot, peer):
        copy = pltpu.make_async_remote_copy(
            src_ref=source, dst_ref=target, send_sem=self.send_sems.at[slot], recv_sem=self.recv_sems.at[slot],
            device_id=peer, device_id_type=MESH,
        )
        copy.start()
        self.sent.append(copy)
        return copy

    def finish(self):
        for copy in self.sent:
            copy.wait_send()
        self.sent = []


class Place:
    def __init__(self):
        self.r = lax.axis_index("region")
        s = lax.axis_index("sub")
        self.y, self.z = lax.rem(s, 4), s // 4
        self.core = lax.rem(self.r, 2)
        self.y1 = self.y + 1 - 2 * lax.rem(self.y, 2)
        self.y3 = 3 - self.y
        self.y2 = lax.rem(self.y + 2, 4)

    def at_y(self, y):
        return {"region": self.r, "sub": self.z * 4 + y}

    def at_z(self, d):
        return {"region": self.r, "sub": lax.rem(self.z + d, 8) * 4 + self.y}

    def at_r(self, r):
        return {"region": r, "sub": self.z * 4 + self.y}


class Reduce:
    def __init__(self, me, copies, x, r1, r2, zbuf, out):
        self.me, self.copies, self.x, self.r1, self.r2, self.zbuf, self.out = me, copies, x, r1, r2, zbuf, out
        self.first = [me.y1, me.y3]
        self.second = [me.y3, me.y1]

    def block(self, ref, h, b):
        return ref.at[h, pl.ds(pl.multiple_of(b * 64, 64), 64), :]

    def start(self):
        me, c = self.me, self.copies
        self.c1 = {}
        for slot in (1, 0):
            for h in (0, 1):
                b = self.first[h] if slot == 0 else me.y2
                self.c1[h, slot] = c.start(self.block(self.x, h, b), self.r1.at[h, slot], c.slots(1), me.at_y(self.first[h]))

    def middle(self):
        me, c = self.me, self.copies
        self.c2 = {}
        for h in (0, 1):
            self.c1[h, 1].wait_recv()
            self.r1[h, 1] = self.r1[h, 1] + self.block(self.x, h, self.second[h])[...]
            self.c2[h] = c.start(self.r1.at[h, 1], self.r2.at[h], c.slots(1), me.at_y(self.second[h]))

    def across(self):
        me, c = self.me, self.copies
        for h in (0, 1):
            self.c1[h, 0].wait_recv()
            self.c2[h].wait_recv()
            self.r1[h, 0] = self.r1[h, 0] + self.block(self.x, h, me.y)[...] + self.r2[h]
        self.cz = []
        for d in (4, 3, 5, 2, 6, 1, 7):
            row = pl.multiple_of(lax.rem(me.z + d, 8) * 8, 8)
            self.cz.append(c.start(self.r1.at[:, 0, pl.ds(row, 8), :], self.zbuf.at[d - 1], c.slots(1), me.at_z(d)))

    def end(self):
        row = pl.multiple_of(self.me.z * 8, 8)
        for copy in self.cz:
            copy.wait_recv()
        for h in (0, 1):
            total = self.r1[h, 0, pl.ds(row, 8), :]
            for d in range(7):
                total = total + self.zbuf[d, h]
            self.out[h] = total


class Gather:
    def __init__(self, me, copies, slab, full):
        self.me, self.copies, self.slab, self.full = me, copies, slab, full

    def block(self, h, b):
        return self.full.at[h, pl.ds(pl.multiple_of(b * 64, 64), 64), :]

    def start(self):
        me, c = self.me, self.copies
        row = pl.multiple_of(me.y * 64 + me.z * 8, 8)
        self.full[:, pl.ds(row, 8), :] = self.slab[...]
        piece = self.full.at[:, pl.ds(row, 8), :]
        self.cz = [c.start(self.slab, piece, c.slots(1), me.at_z(d)) for d in (4, 3, 5, 2, 6, 1, 7)]

    def middle(self):
        me, c = self.me, self.copies
        for copy in self.cz:
            copy.wait_recv()
        self.c1, self.c2 = [], []
        for h, near, far in ((0, me.y3, me.y1), (1, me.y1, me.y3)):
            own = self.block(h, me.y)
            self.c1.append(c.start(own, own, c.slots(1), me.at_y(near)))
            self.c2.append(c.start(own, own, c.slots(1), me.at_y(far)))

    def last(self):
        me, c = self.me, self.copies
        for h, near, far in ((0, me.y3, me.y1), (1, me.y1, me.y3)):
            self.c1[h].wait_recv()
            passed = self.block(h, near)
            self.c2.append(c.start(passed, passed, c.slots(1), me.at_y(far)))

    def end(self):
        for copy in self.c2:
            copy.wait_recv()


class RootSum:
    def __init__(self, me, copies, slab, rx, own, full):
        self.me, self.copies, self.slab, self.rx, self.own, self.full = me, copies, slab, rx, own, full

    def run(self):
        me, c = self.me, self.copies
        slot = c.slots(8)
        for d in range(1, 8):
            peer = lax.rem(me.r + d, 8)
            copy = pltpu.make_async_remote_copy(
                src_ref=self.slab.at[lax.rem(peer, 2)], dst_ref=self.rx.at[me.r],
                send_sem=c.send_sems.at[slot + d - 1], recv_sem=c.recv_sems.at[slot + me.r],
                device_id=me.at_r(peer), device_id_type=MESH,
            )
            copy.start()
            c.sent.append(copy)
        self.rx[me.r] = self.slab[me.core]
        for d in range(1, 8):
            peer = lax.rem(me.r + d, 8)
            pltpu.make_async_remote_copy(
                src_ref=self.slab.at[0], dst_ref=self.rx.at[peer],
                send_sem=c.send_sems.at[slot + d - 1], recv_sem=c.recv_sems.at[slot + peer],
                device_id=me.at_r(peer), device_id_type=MESH,
            ).wait_recv()
        total = self.rx[0]
        for i in range(1, 8):
            total = total + self.rx[i]
        self.own[...] = total
        row = pl.multiple_of(me.y * 64 + me.z * 8, 8)
        self.full[me.core, pl.ds(row, 8), :] = total
        piece = self.full.at[me.core, pl.ds(row, 8), :]
        cz = [c.start(self.own, piece, c.slots(1), me.at_z(d)) for d in (4, 3, 5, 2, 6, 1, 7)]
        for copy in cz:
            copy.wait_recv()
        near = me.y3 + me.core * (me.y1 - me.y3)
        far = me.y1 + me.core * (me.y3 - me.y1)
        sibling = me.at_r(me.r + 1 - 2 * me.core)

        def block(b):
            return self.full.at[me.core, pl.ds(pl.multiple_of(b * 64, 64), 64), :]

        own = block(me.y)
        c1 = c.start(own, own, c.slots(1), me.at_y(near))
        c2 = c.start(own, own, c.slots(1), me.at_y(far))
        cs = [c.start(own, own, c.slots(1), sibling)]
        c1.wait_recv()
        passed = block(near)
        c3 = c.start(passed, passed, c.slots(1), me.at_y(far))
        cs.append(c.start(passed, passed, c.slots(1), sibling))
        c2.wait_recv()
        cs.append(c.start(block(far), block(far), c.slots(1), sibling))
        c3.wait_recv()
        cs.append(c.start(block(me.y2), block(me.y2), c.slots(1), sibling))
        for copy in cs:
            copy.wait_recv()


def both(ref, cols):
    return jnp.concatenate([ref[0, :, cols], ref[1, :, cols]], axis=0)


def main_kernel(
    rows_ref, obs, b0, b1, noise, root_prior, region_prior, root_out, region_low,
    xa, xb, xc, w0, w1, r1a, r2a, za, sa, fa, r1b, r2b, zb, sb, fb, r1c, r2c, zc, sc, slab, rx, own, full,
    inv_a, inv_d, x0, send_sems, recv_sems,
):
    me = Place()
    copies = Copies(send_sems, recv_sems)
    barrier = pltpu.get_barrier_semaphore()
    for peer in [me.at_y(me.y1), me.at_y(me.y3)] + [me.at_z(d) for d in range(1, 8)] + [
        me.at_r(lax.rem(me.r + d, 8)) for d in range(1, 8)
    ]:
        pl.semaphore_signal(barrier, inc=1, device_id=peer, device_id_type=MESH)

    count = rows_ref[0]
    lane = lax.broadcasted_iota(jnp.int32, (1, 128), 1)
    for g in range(8):
        wrow = jnp.where(lane + 128 * g < count, noise[g:g + 1, :], 0.0)
        wt = jnp.broadcast_to(wrow, (128, 128)).T
        for q in range(4):
            rows, cols = slice(128 * g, 128 * g + 128), slice(128 * q, 128 * q + 128)
            w1[rows, cols] = (b1[rows, cols].astype(F32) * wt).astype(BF16)
            w0[rows, cols] = (b0[rows, cols].astype(F32) * wt).astype(BF16)

    def dot(a, b):
        return lax.dot_general(a, b, (TN, ((), ())), preferred_element_type=F32)

    for h in (0, 1):
        half = slice(256 * h, 256 * h + 256)
        xa[h] = 0.5 * (dot(w1[:, half], b1[...]) + dot(b1[:, half], w1[...]))
    pl.semaphore_wait(barrier, 16)
    red_a = Reduce(me, copies, xa, r1a, r2a, za, sa)
    red_a.start()
    for h in (0, 1):
        half = slice(256 * h, 256 * h + 256)
        xb[h, :, :512] = dot(w0[:, half], b1[...])
        xb[h, :, 512:] = dot(w1[:, half], obs[...])
    red_a.middle()
    red_b = Reduce(me, copies, xb, r1b, r2b, zb, sb)
    red_b.start()
    for h in (0, 1):
        half = slice(256 * h, 256 * h + 256)
        xc[h, :, :512] = 0.5 * (dot(w0[:, half], b0[...]) + dot(b0[:, half], w0[...]))
        xc[h, :, 512:] = dot(w0[:, half], obs[...])
    red_a.across()
    red_c = Reduce(me, copies, xc, r1c, r2c, zc, sc)
    red_c.start()
    red_b.middle()
    red_a.end()
    gat_a = Gather(me, copies, sa, fa)
    gat_a.start()
    red_b.across()
    red_c.middle()
    gat_a.middle()
    gat_a.last()
    red_b.end()
    gat_b = Gather(me, copies, sb, fb)
    gat_b.start()
    red_c.across()
    gat_a.end()
    for h in (0, 1):
        half = slice(256 * h, 256 * h + 256)
        inv_a[half, :] = region_prior[half, :] + fa[h]

    def serve(k):
        if k == 0:
            gat_b.middle()
        elif k == 1:
            gat_b.last()
        elif k == 2:
            red_c.end()
            gat_b.end()

    spd_inverse(inv_a, inv_d, serve=serve)
    P3 = split(-inv_a[...])
    u = dot3(split(sb[...].reshape(16, 768)[:, :512]), P3, MM)
    u3 = split(u)
    a01 = split(both(fb, slice(0, 512)))
    w13 = split(both(fb, slice(512, 768)))
    s = sc[...].reshape(16, 768)[:, :512] - dot3(u3, a01, NT)
    t = sc[...].reshape(16, 768)[:, 512:] - dot3(u3, w13, MM)
    slab[:, :, :512] = s.reshape(2, 8, 512)
    slab[:, :, 512:] = t.reshape(2, 8, 256)
    root = RootSum(me, copies, slab, rx, own, full)
    root.run()
    x0[:, :512] = dot3(P3, a01, NT)
    x0[:, 512:] = dot3(P3, w13, MM)
    for h in (0, 1):
        half = slice(256 * h, 256 * h + 256)
        inv_a[half, :] = root_prior[half, :] + full[h, :, :512]
    spd_inverse(inv_a, inv_d)
    mean = dot3(split(-inv_a[...]), split(both(full, slice(512, 768))), MM)
    root_out[...] = mean
    region_low[...] = (x0[:, 512:] - dot3(split(x0[:, :512]), split(mean), MM)).astype(BF16)
    copies.finish()


def estimate(observations, basis_root, basis_region, noise_weights, leaf_rows, root_prior, region_prior):
    vm = lambda *shape: pltpu.VMEM(shape, F32)

    def reduce_set(w):
        return [vm(2, 2, 64, w), vm(2, 64, w), vm(7, 2, 8, w), vm(2, 8, w)]

    spec = pl.BlockSpec(memory_space=pltpu.VMEM)
    return pl.pallas_call(
        main_kernel,
        out_shape=(jax.ShapeDtypeStruct((512, 256), F32), jax.ShapeDtypeStruct((512, 256), BF16)),
        in_specs=[pl.BlockSpec(memory_space=pltpu.SMEM)] + [spec] * 6,
        out_specs=(spec, spec),
        scratch_shapes=[vm(2, 256, 512), vm(2, 256, 768), vm(2, 256, 768),
                        pltpu.VMEM((1024, 512), BF16), pltpu.VMEM((1024, 512), BF16)]
        + reduce_set(512) + [vm(2, 256, 512)] + reduce_set(768) + [vm(2, 256, 768)] + reduce_set(768)
        + [vm(2, 8, 768), vm(8, 8, 768), vm(8, 768), vm(2, 256, 768)]
        + [vm(512, 512), vm(128, 128), vm(512, 768)]
        + [pltpu.SemaphoreType.DMA((100,)), pltpu.SemaphoreType.DMA((100,))],
        compiler_params=pltpu.CompilerParams(collective_id=0, has_side_effects=True, vmem_limit_bytes=60 << 20),
    )(leaf_rows, observations, basis_root, basis_region, noise_weights.reshape(8, 128), root_prior, region_prior[0])


def body(
    observations, basis_root, basis_region, noise_weights, leaf_rows, root_prior, region_prior
):
    root_mean, region_low = estimate(
        observations, basis_root, basis_region, noise_weights, leaf_rows, root_prior, region_prior
    )
    fitted = jnp.dot(basis_root, root_mean.astype(jnp.bfloat16), preferred_element_type=jnp.float32)
    fitted = fitted + jnp.dot(basis_region, region_low, preferred_element_type=jnp.float32)
    return (fitted, root_mean)


def solution(mesh):
    placed = (
        P(("region", "sub"), None),
        P(("region", "sub"), None),
        P(("region", "sub"), None),
        P(("region", "sub")),
        P(("region", "sub")),
        P(),
        P("region", None, None),
    )
    return jax.shard_map(
        body,
        mesh=mesh,
        in_specs=placed,
        out_specs=(P(("region", "sub"), None), P()),
        check_vma=False,
    )
```

```python
import functools

import jax
import jax.numpy as jnp
from jax import lax
from jax.experimental import pallas as pl
from jax.experimental.pallas import tpu as pltpu
from jax.sharding import PartitionSpec as P

MESH = pl.DeviceIdType.MESH
F32 = jnp.float32
BF16 = jnp.bfloat16
HI = lax.Precision.HIGHEST

def split(x):
    hi = x.astype(BF16)
    return hi, (x - hi.astype(F32)).astype(BF16)

def dot3(a, b, dims):
    ah, al = a
    bh, bl = b
    d = lambda u, v: lax.dot_general(u, v, (dims, ((), ())), preferred_element_type=F32)
    return d(ah, bh) + (d(ah, bl) + d(al, bh))

MM = ((1,), (0,))

def inv_small(s):
    s = dict(s)
    g = lambda i, j: s[(i, j)] if i >= j else s[(j, i)]
    for k in range(0, 8, 2):
        a, b, c = g(k, k), g(k + 1, k), g(k + 1, k + 1)
        r = 1.0 / (a * c - b * b)
        d00, d01, d11 = c * r, -b * r, a * r
        others = [i for i in range(8) if i not in (k, k + 1)]
        t = {}
        for i in others:
            u, v = g(i, k), g(i, k + 1)
            t[i] = (u * d00 + v * d01, u * d01 + v * d11)
        new = {}
        for i in others:
            for j in others:
                if i >= j:
                    new[(i, j)] = g(i, j) - (t[i][0] * g(j, k) + t[i][1] * g(j, k + 1))
        for i in others:
            for q in (0, 1):
                key = (max(i, k + q), min(i, k + q))
                new[key] = t[i][q]
        new[(k, k)], new[(k + 1, k)], new[(k + 1, k + 1)] = -d00, -d01, -d11
        s = new
    return {key: -v for key, v in s.items()}

def inv128(rows, tmp, serve=None, base=0):
    lane = lax.broadcasted_iota(jnp.int32, (8, 128), 1)
    sub = lax.broadcasted_iota(jnp.int32, (8, 128), 0)
    a = list(rows)
    for p in range(16):
        if serve is not None:
            serve(base + p)
        R = a[p]
        k0 = 8 * p
        inK = (lane >= k0) & (lane < k0 + 8)
        cols = [jnp.broadcast_to(R[:, k0 + j:k0 + j + 1], (8, 128)) for j in range(8)]
        for j in range(8):
            tmp[8 * j:8 * j + 8, :] = cols[j]
        s = {(i, j): tmp[pl.ds(8 * j + i, 8, stride=0), :] for i in range(8) for j in range(i + 1)}
        Rm = jnp.where(inK, jnp.where(lane - k0 == sub, -1.0, 0.0), R)
        tmp[64:72, :] = Rm
        Rb = [tmp[pl.ds(64 + q, 8, stride=0), :] for q in range(8)]
        D = inv_small(s)
        g = lambda i, j: D[(i, j)] if i >= j else D[(j, i)]
        G = []
        for i in range(8):
            t = [g(i, q) * Rb[q] for q in range(8)]
            while len(t) > 1:
                t = [t[m] + t[m + 1] for m in range(0, len(t), 2)]
            G.append(t[0])
        new = G[7]
        for q in range(7):
            new = jnp.where(sub == q, G[q], new)
        Rh, Gh = R.astype(BF16).astype(F32), new.astype(BF16).astype(F32)
        Rl, Gl = R - Rh, new - Gh
        left = jnp.concatenate([Rh, Rh, Rl, Rl], axis=0).astype(BF16)
        right = jnp.concatenate([Gh, Gl, Gh, Gl], axis=0).astype(BF16)
        if p < 15:
            i = p + 1
            c = [jnp.broadcast_to(a[i][:, k0 + j:k0 + j + 1], (8, 128)) * G[j] for j in range(8)]
            while len(c) > 1:
                c = [c[m] + c[m + 1] for m in range(0, len(c), 2)]
            a[i] = jnp.where(inK, 0.0, a[i]) - c[0]
        U = lax.dot_general(left, right, (((0,), (0,)), ((), ())), preferred_element_type=F32)
        for i in range(16):
            if i != p and i != p + 1:
                a[i] = jnp.where(inK, 0.0, a[i]) - U[8 * i:8 * i + 8, :]
        a[p] = new
    return a

def spd_inverse(A, Dbuf, n=512, serve=None):
    nb = n // 128
    def step(k, carry):
        o = k * 128 if serve is not None else pl.multiple_of(k * 128, 128)
        rows = [A[pl.ds(o + 8 * i if serve is not None else pl.multiple_of(o + 8 * i, 8), 8), pl.ds(o, 128)] for i in range(16)]
        out = inv128(rows, Dbuf, serve, 16 * k)
        for i in range(16):
            Dbuf[8 * i:8 * i + 8, :] = -out[i]
        D = split(Dbuf[...])
        Rk = split(A[pl.ds(o, 128), :])
        Ck = split(A[:, pl.ds(o, 128)])
        G = dot3(D, Rk, MM)
        T = dot3(Ck, D, MM)
        U = dot3(Ck, split(G), MM)
        A[...] = A[...] - U
        A[pl.ds(o, 128), :] = G
        A[:, pl.ds(o, 128)] = T
        A[pl.ds(o, 128), pl.ds(o, 128)] = -Dbuf[...]
        return carry
    if serve is None:
        lax.fori_loop(0, nb, step, 0)
    else:
        for k in range(nb):
            step(k, 0)


NT = ((1,), (1,))
TN = ((0,), (0,))


class Copies:
    def __init__(self, send_sems, recv_sems):
        self.send_sems, self.recv_sems, self.used, self.sent = send_sems, recv_sems, 0, []

    def slots(self, count):
        first = self.used
        self.used += count
        return first

    def start(self, source, target, slot, peer):
        copy = pltpu.make_async_remote_copy(
            src_ref=source, dst_ref=target, send_sem=self.send_sems.at[slot], recv_sem=self.recv_sems.at[slot],
            device_id=peer, device_id_type=MESH,
        )
        copy.start()
        self.sent.append(copy)
        return copy

    def finish(self):
        for copy in self.sent:
            copy.wait_send()
        self.sent = []


class Place:
    def __init__(self):
        self.r = lax.axis_index("region")
        s = lax.axis_index("sub")
        self.y, self.z = lax.rem(s, 4), s // 4
        self.core = lax.rem(self.r, 2)
        self.y1 = self.y + 1 - 2 * lax.rem(self.y, 2)
        self.y3 = 3 - self.y
        self.y2 = lax.rem(self.y + 2, 4)

    def at_y(self, y):
        return {"region": self.r, "sub": self.z * 4 + y}

    def at_z(self, d):
        return {"region": self.r, "sub": lax.rem(self.z + d, 8) * 4 + self.y}

    def at_r(self, r):
        return {"region": r, "sub": self.z * 4 + self.y}


class Reduce:
    def __init__(self, me, copies, x, r1, r2, zbuf, out):
        self.me, self.copies, self.x, self.r1, self.r2, self.zbuf, self.out = me, copies, x, r1, r2, zbuf, out
        self.first = [me.y1, me.y3]
        self.second = [me.y3, me.y1]

    def block(self, ref, h, b):
        return ref.at[h, pl.ds(pl.multiple_of(b * 64, 64), 64), :]

    def start(self):
        me, c = self.me, self.copies
        self.c1 = {}
        for slot in (1, 0):
            for h in (0, 1):
                b = self.first[h] if slot == 0 else me.y2
                self.c1[h, slot] = c.start(self.block(self.x, h, b), self.r1.at[h, slot], c.slots(1), me.at_y(self.first[h]))

    def middle(self):
        me, c = self.me, self.copies
        self.c2 = {}
        for h in (0, 1):
            self.c1[h, 1].wait_recv()
            self.r1[h, 1] = self.r1[h, 1] + self.block(self.x, h, self.second[h])[...]
            self.c2[h] = c.start(self.r1.at[h, 1], self.r2.at[h], c.slots(1), me.at_y(self.second[h]))

    def across(self):
        me, c = self.me, self.copies
        for h in (0, 1):
            self.c1[h, 0].wait_recv()
            self.c2[h].wait_recv()
            self.r1[h, 0] = self.r1[h, 0] + self.block(self.x, h, me.y)[...] + self.r2[h]
        self.cz = [[], []]
        self.c_step(0)

    def chunk(self, d):
        row = pl.multiple_of(lax.rem(self.me.z + d + 8, 8) * 8, 8)
        return self.r1.at[:, 0, pl.ds(row, 8), :]

    def c_step(self, step):
        me, c = self.me, self.copies
        for side, way in ((0, 1), (1, -1)):
            part = self.chunk(way * (4 - step))
            slot = 4 * side + step
            if step == 0:
                source, target = part.at[side], self.zbuf.at[slot, side]
            else:
                source, target = part, self.zbuf.at[slot]
            self.cz[side].append(c.start(source, target, c.slots(1), me.at_z(1 if side == 0 else 7)))

    def pass_on(self, step):
        for side, way in ((0, 1), (1, -1)):
            self.cz[side][step - 1].wait_recv()
            part, slot = self.chunk(way * (4 - step)), 4 * side + step - 1
            if step == 1:
                part[side] = part[side] + self.zbuf[slot, side]
            else:
                part[...] = part[...] + self.zbuf[slot]
        self.c_step(step)

    def end(self):
        for side in (0, 1):
            self.cz[side][3].wait_recv()
        self.out[...] = self.chunk(0)[...] + self.zbuf[3] + self.zbuf[7]


class Gather:
    def __init__(self, me, copies, slab, full):
        self.me, self.copies, self.slab, self.full = me, copies, slab, full

    def block(self, h, b):
        return self.full.at[h, pl.ds(pl.multiple_of(b * 64, 64), 64), :]

    def start(self):
        me, c = self.me, self.copies
        row = pl.multiple_of(me.y * 64 + me.z * 8, 8)
        self.full[:, pl.ds(row, 8), :] = self.slab[...]
        self.cz = [[], []]
        self.send(0)

    def send(self, step):
        me, c = self.me, self.copies
        for side, way in ((0, -1), (1, 1)):
            row = pl.multiple_of(me.y * 64 + lax.rem(me.z + way * step + 8, 8) * 8, 8)
            piece = self.full.at[:, pl.ds(row, 8), :]
            if step == 3:
                piece = piece.at[side]
            self.cz[side].append(c.start(piece, piece, c.slots(1), me.at_z(1 if side == 0 else 7)))

    def pass_on(self, step):
        for side in (0, 1):
            self.cz[side][step - 1].wait_recv()
        self.send(step)

    def middle(self):
        me, c = self.me, self.copies
        for side in (0, 1):
            self.cz[side][3].wait_recv()
        self.c1, self.c2 = [], []
        for h, near, far in ((0, me.y3, me.y1), (1, me.y1, me.y3)):
            own = self.block(h, me.y)
            self.c1.append(c.start(own, own, c.slots(1), me.at_y(near)))
            self.c2.append(c.start(own, own, c.slots(1), me.at_y(far)))

    def last(self):
        me, c = self.me, self.copies
        for h, near, far in ((0, me.y3, me.y1), (1, me.y1, me.y3)):
            self.c1[h].wait_recv()
            passed = self.block(h, near)
            self.c2.append(c.start(passed, passed, c.slots(1), me.at_y(far)))

    def end(self):
        for copy in self.c2:
            copy.wait_recv()


class RootSum:
    def __init__(self, me, copies, slab, rx, own, full):
        self.me, self.copies, self.slab, self.rx, self.own, self.full = me, copies, slab, rx, own, full

    def run(self, fill):
        me, c = self.me, self.copies
        slot = c.slots(8)
        for d in range(1, 8):
            peer = lax.rem(me.r + d, 8)
            copy = pltpu.make_async_remote_copy(
                src_ref=self.slab.at[lax.rem(peer, 2)], dst_ref=self.rx.at[me.r],
                send_sem=c.send_sems.at[slot + d - 1], recv_sem=c.recv_sems.at[slot + me.r],
                device_id=me.at_r(peer), device_id_type=MESH,
            )
            copy.start()
            c.sent.append(copy)
        self.rx[me.r] = self.slab[me.core]
        for d in range(1, 8):
            peer = lax.rem(me.r + d, 8)
            pltpu.make_async_remote_copy(
                src_ref=self.slab.at[0], dst_ref=self.rx.at[peer],
                send_sem=c.send_sems.at[slot + d - 1], recv_sem=c.recv_sems.at[slot + peer],
                device_id=me.at_r(peer), device_id_type=MESH,
            ).wait_recv()
        total = self.rx[0]
        for i in range(1, 8):
            total = total + self.rx[i]
        self.own[...] = total
        row = pl.multiple_of(me.y * 64 + me.z * 8, 8)
        self.full[me.core, pl.ds(row, 8), :] = total
        piece = self.full.at[me.core, pl.ds(row, 8), :]
        cz = [c.start(self.own, piece, c.slots(1), me.at_z(d)) for d in (4, 3, 5, 2, 6, 1, 7)]
        fill(0)
        for copy in cz:
            copy.wait_recv()
        near = me.y3 + me.core * (me.y1 - me.y3)
        far = me.y1 + me.core * (me.y3 - me.y1)
        sibling = me.at_r(me.r + 1 - 2 * me.core)

        def block(b):
            return self.full.at[me.core, pl.ds(pl.multiple_of(b * 64, 64), 64), :]

        own = block(me.y)
        c1 = c.start(own, own, c.slots(1), me.at_y(near))
        c2 = c.start(own, own, c.slots(1), me.at_y(far))
        cs = [c.start(own, own, c.slots(1), sibling)]
        fill(1)
        c1.wait_recv()
        passed = block(near)
        c3 = c.start(passed, passed, c.slots(1), me.at_y(far))
        cs.append(c.start(passed, passed, c.slots(1), sibling))
        c2.wait_recv()
        cs.append(c.start(block(far), block(far), c.slots(1), sibling))
        c3.wait_recv()
        cs.append(c.start(block(me.y2), block(me.y2), c.slots(1), sibling))
        for copy in cs:
            copy.wait_recv()


def both(ref, cols):
    return jnp.concatenate([ref[0, :, cols], ref[1, :, cols]], axis=0)


def main_kernel(
    rows_ref, obs, b0, b1, noise, root_prior, region_prior, root_out, region_low,
    xa, xb, xc, w0, w1, r1a, r2a, za, sa, fa, r1b, r2b, zb, sb, fb, r1c, r2c, zc, sc, slab, rx, own, full,
    inv_a, inv_d, x0, send_sems, recv_sems,
):
    me = Place()
    copies = Copies(send_sems, recv_sems)
    barrier = pltpu.get_barrier_semaphore()
    for peer in [me.at_y(me.y1), me.at_y(me.y3)] + [me.at_z(d) for d in range(1, 8)] + [
        me.at_r(lax.rem(me.r + d, 8)) for d in range(1, 8)
    ]:
        pl.semaphore_signal(barrier, inc=1, device_id=peer, device_id_type=MESH)

    count = rows_ref[0]
    lane = lax.broadcasted_iota(jnp.int32, (1, 128), 1)
    for g in range(8):
        wrow = jnp.where(lane + 128 * g < count, noise[g:g + 1, :], 0.0)
        wt = jnp.broadcast_to(wrow, (128, 128)).T
        for q in range(4):
            rows, cols = slice(128 * g, 128 * g + 128), slice(128 * q, 128 * q + 128)
            w1[rows, cols] = (b1[rows, cols].astype(F32) * wt).astype(BF16)
            w0[rows, cols] = (b0[rows, cols].astype(F32) * wt).astype(BF16)

    def dot(a, b):
        return lax.dot_general(a, b, (TN, ((), ())), preferred_element_type=F32)

    for h in (0, 1):
        half = slice(256 * h, 256 * h + 256)
        xa[h] = 0.5 * (dot(w1[:, half], b1[...]) + dot(b1[:, half], w1[...]))
    pl.semaphore_wait(barrier, 16)
    red_a = Reduce(me, copies, xa, r1a, r2a, za, sa)
    red_a.start()
    for h in (0, 1):
        half = slice(256 * h, 256 * h + 256)
        xb[h, :, :512] = dot(w0[:, half], b1[...])
        xb[h, :, 512:] = dot(w1[:, half], obs[...])
    red_a.middle()
    red_b = Reduce(me, copies, xb, r1b, r2b, zb, sb)
    red_b.start()
    for h in (0, 1):
        half = slice(256 * h, 256 * h + 256)
        xc[h, :, :512] = 0.5 * (dot(w0[:, half], b0[...]) + dot(b0[:, half], w0[...]))
        xc[h, :, 512:] = dot(w0[:, half], obs[...])
    red_c = Reduce(me, copies, xc, r1c, r2c, zc, sc)
    red_a.across()
    for step in (1, 2, 3):
        red_a.pass_on(step)
    red_a.end()
    gat_a = Gather(me, copies, sa, fa)
    gat_b = Gather(me, copies, sb, fb)
    gat_a.start()
    red_b.middle()
    red_c.start()
    for step in (1, 2, 3):
        gat_a.pass_on(step)
    gat_a.middle()
    red_b.across()
    red_b.pass_on(1)
    gat_a.last()
    red_b.pass_on(2)
    gat_a.end()
    for h in (0, 1):
        half = slice(256 * h, 256 * h + 256)
        inv_a[half, :] = region_prior[half, :] + fa[h]
    tasks = {
        2: [lambda: red_b.pass_on(3)],
        6: [red_c.middle],
        10: [red_b.end, gat_b.start],
        18: [lambda: gat_b.pass_on(1)],
        25: [red_c.across, lambda: gat_b.pass_on(2)],
        33: [lambda: red_c.pass_on(1), lambda: gat_b.pass_on(3)],
        41: [gat_b.middle, lambda: red_c.pass_on(2)],
        50: [lambda: red_c.pass_on(3)],
        58: [gat_b.last, red_c.end],
    }

    def serve(point):
        for task in tasks.get(point, []):
            task()

    spd_inverse(inv_a, inv_d, serve=serve)
    P3 = split(-inv_a[...])
    u = dot3(split(sb[...].reshape(16, 768)[:, :512]), P3, MM)
    u3 = split(u)
    gat_b.end()
    a01 = split(both(fb, slice(0, 512)))
    w13 = split(both(fb, slice(512, 768)))
    s = sc[...].reshape(16, 768)[:, :512] - dot3(u3, a01, NT)
    t = sc[...].reshape(16, 768)[:, 512:] - dot3(u3, w13, MM)
    slab[:, :, :512] = s.reshape(2, 8, 512)
    slab[:, :, 512:] = t.reshape(2, 8, 256)
    root = RootSum(me, copies, slab, rx, own, full)

    def fill(part):
        if part == 0:
            x0[:, :512] = dot3(P3, a01, NT)
        else:
            x0[:, 512:] = dot3(P3, w13, MM)

    root.run(fill)
    for h in (0, 1):
        half = slice(256 * h, 256 * h + 256)
        inv_a[half, :] = root_prior[half, :] + full[h, :, :512]
    spd_inverse(inv_a, inv_d)
    mean = dot3(split(-inv_a[...]), split(both(full, slice(512, 768))), MM)
    root_out[...] = mean
    region_low[...] = (x0[:, 512:] - dot3(split(x0[:, :512]), split(mean), MM)).astype(BF16)
    copies.finish()


def estimate(observations, basis_root, basis_region, noise_weights, leaf_rows, root_prior, region_prior):
    vm = lambda *shape: pltpu.VMEM(shape, F32)

    def reduce_set(w):
        return [vm(2, 2, 64, w), vm(2, 64, w), vm(8, 2, 8, w), vm(2, 8, w)]

    spec = pl.BlockSpec(memory_space=pltpu.VMEM)
    return pl.pallas_call(
        main_kernel,
        out_shape=(jax.ShapeDtypeStruct((512, 256), F32), jax.ShapeDtypeStruct((512, 256), BF16)),
        in_specs=[pl.BlockSpec(memory_space=pltpu.SMEM)] + [spec] * 6,
        out_specs=(spec, spec),
        scratch_shapes=[vm(2, 256, 512), vm(2, 256, 768), vm(2, 256, 768),
                        pltpu.VMEM((1024, 512), BF16), pltpu.VMEM((1024, 512), BF16)]
        + reduce_set(512) + [vm(2, 256, 512)] + reduce_set(768) + [vm(2, 256, 768)] + reduce_set(768)
        + [vm(2, 8, 768), vm(8, 8, 768), vm(8, 768), vm(2, 256, 768)]
        + [vm(512, 512), vm(128, 128), vm(512, 768)]
        + [pltpu.SemaphoreType.DMA((112,)), pltpu.SemaphoreType.DMA((112,))],
        compiler_params=pltpu.CompilerParams(collective_id=0, has_side_effects=True, vmem_limit_bytes=60 << 20),
    )(leaf_rows, observations, basis_root, basis_region, noise_weights.reshape(8, 128), root_prior, region_prior[0])


def body(
    observations, basis_root, basis_region, noise_weights, leaf_rows, root_prior, region_prior
):
    root_mean, region_low = estimate(
        observations, basis_root, basis_region, noise_weights, leaf_rows, root_prior, region_prior
    )
    fitted = jnp.dot(basis_root, root_mean.astype(jnp.bfloat16), preferred_element_type=jnp.float32)
    fitted = fitted + jnp.dot(basis_region, region_low, preferred_element_type=jnp.float32)
    return (fitted, root_mean)


def solution(mesh):
    placed = (
        P(("region", "sub"), None),
        P(("region", "sub"), None),
        P(("region", "sub"), None),
        P(("region", "sub")),
        P(("region", "sub")),
        P(),
        P("region", None, None),
    )
    return jax.shard_map(
        body,
        mesh=mesh,
        in_specs=placed,
        out_specs=(P(("region", "sub"), None), P()),
        check_vma=False,
    )
```

```python
import functools

import jax
import jax.numpy as jnp
from jax import lax
from jax.experimental import pallas as pl
from jax.experimental.pallas import tpu as pltpu
from jax.sharding import PartitionSpec as P

MESH = pl.DeviceIdType.MESH
F32 = jnp.float32
BF16 = jnp.bfloat16
HI = lax.Precision.HIGHEST

def split(x):
    hi = x.astype(BF16)
    return hi, (x - hi.astype(F32)).astype(BF16)

def dot3(a, b, dims):
    ah, al = a
    bh, bl = b
    d = lambda u, v: lax.dot_general(u, v, (dims, ((), ())), preferred_element_type=F32)
    return d(ah, bh) + (d(ah, bl) + d(al, bh))

MM = ((1,), (0,))

def inv_small(s):
    s = dict(s)
    g = lambda i, j: s[(i, j)] if i >= j else s[(j, i)]
    for k in range(0, 8, 2):
        a, b, c = g(k, k), g(k + 1, k), g(k + 1, k + 1)
        r = 1.0 / (a * c - b * b)
        d00, d01, d11 = c * r, -b * r, a * r
        others = [i for i in range(8) if i not in (k, k + 1)]
        t = {}
        for i in others:
            u, v = g(i, k), g(i, k + 1)
            t[i] = (u * d00 + v * d01, u * d01 + v * d11)
        new = {}
        for i in others:
            for j in others:
                if i >= j:
                    new[(i, j)] = g(i, j) - (t[i][0] * g(j, k) + t[i][1] * g(j, k + 1))
        for i in others:
            for q in (0, 1):
                key = (max(i, k + q), min(i, k + q))
                new[key] = t[i][q]
        new[(k, k)], new[(k + 1, k)], new[(k + 1, k + 1)] = -d00, -d01, -d11
        s = new
    return {key: -v for key, v in s.items()}

def inv128(rows, tmp, serve=None, base=0):
    lane = lax.broadcasted_iota(jnp.int32, (8, 128), 1)
    sub = lax.broadcasted_iota(jnp.int32, (8, 128), 0)
    a = list(rows)
    for p in range(16):
        if serve is not None:
            serve(base + p)
        R = a[p]
        k0 = 8 * p
        inK = (lane >= k0) & (lane < k0 + 8)
        cols = [jnp.broadcast_to(R[:, k0 + j:k0 + j + 1], (8, 128)) for j in range(8)]
        for j in range(8):
            tmp[8 * j:8 * j + 8, :] = cols[j]
        s = {(i, j): tmp[pl.ds(8 * j + i, 8, stride=0), :] for i in range(8) for j in range(i + 1)}
        Rm = jnp.where(inK, jnp.where(lane - k0 == sub, -1.0, 0.0), R)
        tmp[64:72, :] = Rm
        Rb = [tmp[pl.ds(64 + q, 8, stride=0), :] for q in range(8)]
        D = inv_small(s)
        g = lambda i, j: D[(i, j)] if i >= j else D[(j, i)]
        G = []
        for i in range(8):
            t = [g(i, q) * Rb[q] for q in range(8)]
            while len(t) > 1:
                t = [t[m] + t[m + 1] for m in range(0, len(t), 2)]
            G.append(t[0])
        new = G[7]
        for q in range(7):
            new = jnp.where(sub == q, G[q], new)
        Rh, Gh = R.astype(BF16).astype(F32), new.astype(BF16).astype(F32)
        Rl, Gl = R - Rh, new - Gh
        left = jnp.concatenate([Rh, Rh, Rl, Rl], axis=0).astype(BF16)
        right = jnp.concatenate([Gh, Gl, Gh, Gl], axis=0).astype(BF16)
        if p < 15:
            i = p + 1
            c = [jnp.broadcast_to(a[i][:, k0 + j:k0 + j + 1], (8, 128)) * G[j] for j in range(8)]
            while len(c) > 1:
                c = [c[m] + c[m + 1] for m in range(0, len(c), 2)]
            a[i] = jnp.where(inK, 0.0, a[i]) - c[0]
        U = lax.dot_general(left, right, (((0,), (0,)), ((), ())), preferred_element_type=F32)
        for i in range(16):
            if i != p and i != p + 1:
                a[i] = jnp.where(inK, 0.0, a[i]) - U[8 * i:8 * i + 8, :]
        a[p] = new
    return a

def spd_inverse(A, Dbuf, n=512, serve=None):
    nb = n // 128
    def step(k, carry):
        o = k * 128 if serve is not None else pl.multiple_of(k * 128, 128)
        rows = [A[pl.ds(o + 8 * i if serve is not None else pl.multiple_of(o + 8 * i, 8), 8), pl.ds(o, 128)] for i in range(16)]
        out = inv128(rows, Dbuf, serve, 16 * k)
        for i in range(16):
            Dbuf[8 * i:8 * i + 8, :] = -out[i]
        D = split(Dbuf[...])
        Rk = split(A[pl.ds(o, 128), :])
        Ck = split(A[:, pl.ds(o, 128)])
        G = dot3(D, Rk, MM)
        T = dot3(Ck, D, MM)
        U = dot3(Ck, split(G), MM)
        A[...] = A[...] - U
        A[pl.ds(o, 128), :] = G
        A[:, pl.ds(o, 128)] = T
        A[pl.ds(o, 128), pl.ds(o, 128)] = -Dbuf[...]
        return carry
    if serve is None:
        lax.fori_loop(0, nb, step, 0)
    else:
        for k in range(nb):
            step(k, 0)


NT = ((1,), (1,))
TN = ((0,), (0,))


class Copies:
    def __init__(self, send_sems, recv_sems):
        self.send_sems, self.recv_sems, self.used, self.sent = send_sems, recv_sems, 0, []

    def slots(self, count):
        first = self.used
        self.used += count
        return first

    def start(self, source, target, slot, peer):
        copy = pltpu.make_async_remote_copy(
            src_ref=source, dst_ref=target, send_sem=self.send_sems.at[slot], recv_sem=self.recv_sems.at[slot],
            device_id=peer, device_id_type=MESH,
        )
        copy.start()
        self.sent.append(copy)
        return copy

    def finish(self):
        for copy in self.sent:
            copy.wait_send()
        self.sent = []


class Place:
    def __init__(self):
        self.r = lax.axis_index("region")
        s = lax.axis_index("sub")
        self.y, self.z = lax.rem(s, 4), s // 4
        self.core = lax.rem(self.r, 2)
        self.y1 = self.y + 1 - 2 * lax.rem(self.y, 2)
        self.y3 = 3 - self.y
        self.y2 = lax.rem(self.y + 2, 4)

    def at_y(self, y):
        return {"region": self.r, "sub": self.z * 4 + y}

    def at_z(self, d):
        return {"region": self.r, "sub": lax.rem(self.z + d, 8) * 4 + self.y}

    def at_r(self, r):
        return {"region": r, "sub": self.z * 4 + self.y}


class Ring:
    def rows(self, d):
        return pl.ds(pl.multiple_of(lax.rem(self.me.z + d + 8, 8) * 8, 8), 8)

    def up_or_down(self, side):
        return self.me.at_z(1 if side == 0 else 7)


class Reduce(Ring):
    def __init__(self, me, copies, x, cols, y_first, r1, r2, zbuf, part, out):
        self.me, self.copies, self.x, self.cols, self.y_first = me, copies, x, cols, y_first
        self.r1, self.r2, self.zbuf, self.part, self.out = r1, r2, zbuf, part, out
        self.first, self.second = [me.y1, me.y3], [me.y3, me.y1]
        self.c1, self.c2, self.cz = {}, {}, [[], []]
        ring = [self.z_start, lambda: self.z_pass(1), lambda: self.z_pass(2), lambda: self.z_pass(3)]
        if y_first:
            self.steps = [self.y_start, self.y_middle, lambda: (self.y_end(), ring[0]())] + ring[1:] + [self.z_end]
        else:
            self.steps = ring + [lambda: (self.z_end(), self.y_start()), self.y_middle, self.y_end]

    def block(self, h, b):
        return self.x.at[h, b, :, self.cols] if self.y_first else self.part.at[h, b]

    def y_start(self):
        me, c = self.me, self.copies
        for slot in (1, 0):
            for h in (0, 1):
                b = self.first[h] if slot == 0 else me.y2
                self.c1[h, slot] = c.start(self.block(h, b), self.r1.at[h, slot], c.slots(1), me.at_y(self.first[h]))

    def y_middle(self):
        me, c = self.me, self.copies
        for h in (0, 1):
            self.c1[h, 1].wait_recv()
            self.r1[h, 1] = self.r1[h, 1] + self.block(h, self.second[h])[...]
            self.c2[h] = c.start(self.r1.at[h, 1], self.r2.at[h], c.slots(1), me.at_y(self.second[h]))

    def y_end(self):
        for h in (0, 1):
            self.c1[h, 0].wait_recv()
            self.c2[h].wait_recv()
            total = self.r1[h, 0] + self.block(h, self.me.y)[...] + self.r2[h]
            if self.y_first:
                self.r1[h, 0] = total
            else:
                self.out[h, :, self.cols] = total

    def chunk(self, d):
        return self.r1.at[:, 0, self.rows(d), :] if self.y_first else self.x.at[:, :, self.rows(d), self.cols]

    def z_send(self, step):
        c = self.copies
        for side, way in ((0, 1), (1, -1)):
            source, target = self.chunk(way * (4 - step)), self.zbuf.at[4 * side + step]
            if step == 0:
                source, target = source.at[side], target.at[side]
            self.cz[side].append(c.start(source, target, c.slots(1), self.up_or_down(side)))

    def z_start(self):
        self.z_send(0)

    def z_pass(self, step):
        for side, way in ((0, 1), (1, -1)):
            self.cz[side][step - 1].wait_recv()
            part, slot = self.chunk(way * (4 - step)), 4 * side + step - 1
            if step == 1:
                part[side] = part[side] + self.zbuf[slot, side]
            else:
                part[...] = part[...] + self.zbuf[slot]
        self.z_send(step)

    def z_end(self):
        for side in (0, 1):
            self.cz[side][3].wait_recv()
        total = self.chunk(0)[...] + self.zbuf[3] + self.zbuf[7]
        if self.y_first:
            self.out[:, :, self.cols] = total
        else:
            self.part[...] = total


class Gather(Ring):
    def __init__(self, me, copies, slab, full, cols, y_first):
        self.me, self.copies, self.slab, self.full, self.cols, self.y_first = me, copies, slab, full, cols, y_first
        self.c1, self.c2, self.cz = [], [], [[], []]
        ring = [lambda: self.z_send(0), lambda: self.z_pass(1), lambda: self.z_pass(2), lambda: self.z_pass(3)]
        if y_first:
            self.steps = [lambda: (self.place(), self.y_start()), self.y_pass, lambda: (self.y_end(), ring[0]())]
            self.steps += ring[1:] + [self.z_end]
        else:
            self.steps = [lambda: (self.place(), ring[0]())] + ring[1:]
            self.steps += [lambda: (self.z_end(), self.y_start()), self.y_pass, self.y_end]

    def place(self):
        self.full[:, self.me.y, self.rows(0), self.cols] = self.slab[:, :, self.cols]

    def block(self, h, b):
        return self.full.at[h, b, self.rows(0), self.cols] if self.y_first else self.full.at[h, b, :, self.cols]

    def chunk(self, d):
        if self.y_first:
            return self.full.at[:, :, self.rows(d), self.cols]
        return self.full.at[:, self.me.y, self.rows(d), self.cols]

    def y_start(self):
        me, c = self.me, self.copies
        for h, near, far in ((0, me.y3, me.y1), (1, me.y1, me.y3)):
            own = self.block(h, me.y)
            self.c1.append(c.start(own, own, c.slots(1), me.at_y(near)))
            self.c2.append(c.start(own, own, c.slots(1), me.at_y(far)))

    def y_pass(self):
        me, c = self.me, self.copies
        for h, near, far in ((0, me.y3, me.y1), (1, me.y1, me.y3)):
            self.c1[h].wait_recv()
            passed = self.block(h, near)
            self.c2.append(c.start(passed, passed, c.slots(1), me.at_y(far)))

    def y_end(self):
        for copy in self.c2:
            copy.wait_recv()

    def z_send(self, step):
        c = self.copies
        for side, way in ((0, -1), (1, 1)):
            piece = self.chunk(way * step)
            if step == 3:
                piece = piece.at[side]
            self.cz[side].append(c.start(piece, piece, c.slots(1), self.up_or_down(side)))

    def z_pass(self, step):
        for side in (0, 1):
            self.cz[side][step - 1].wait_recv()
        self.z_send(step)

    def z_end(self):
        for side in (0, 1):
            self.cz[side][3].wait_recv()


class Both:
    def __init__(self, *halves):
        self.halves = halves

    def __call__(self, step):
        for half in self.halves:
            half.steps[step]()


class RootSum:
    def __init__(self, me, copies, slab, rx, own, full):
        self.me, self.copies, self.slab, self.rx, self.own, self.full = me, copies, slab, rx, own, full

    def run(self, fill):
        me, c = self.me, self.copies
        slot = c.slots(8)
        for d in range(1, 8):
            peer = lax.rem(me.r + d, 8)
            copy = pltpu.make_async_remote_copy(
                src_ref=self.slab.at[lax.rem(peer, 2)], dst_ref=self.rx.at[me.r],
                send_sem=c.send_sems.at[slot + d - 1], recv_sem=c.recv_sems.at[slot + me.r],
                device_id=me.at_r(peer), device_id_type=MESH,
            )
            copy.start()
            c.sent.append(copy)
        self.rx[me.r] = self.slab[me.core]
        for d in range(1, 8):
            peer = lax.rem(me.r + d, 8)
            pltpu.make_async_remote_copy(
                src_ref=self.slab.at[0], dst_ref=self.rx.at[peer],
                send_sem=c.send_sems.at[slot + d - 1], recv_sem=c.recv_sems.at[slot + peer],
                device_id=me.at_r(peer), device_id_type=MESH,
            ).wait_recv()
        total = self.rx[0]
        for i in range(1, 8):
            total = total + self.rx[i]
        self.own[...] = total
        row = pl.multiple_of(me.y * 64 + me.z * 8, 8)
        self.full[me.core, pl.ds(row, 8), :] = total
        piece = self.full.at[me.core, pl.ds(row, 8), :]
        cz = [c.start(self.own, piece, c.slots(1), me.at_z(d)) for d in (4, 3, 5, 2, 6, 1, 7)]
        fill(0)
        for copy in cz:
            copy.wait_recv()
        near = me.y3 + me.core * (me.y1 - me.y3)
        far = me.y1 + me.core * (me.y3 - me.y1)
        sibling = me.at_r(me.r + 1 - 2 * me.core)

        def block(b):
            return self.full.at[me.core, pl.ds(pl.multiple_of(b * 64, 64), 64), :]

        own = block(me.y)
        c1 = c.start(own, own, c.slots(1), me.at_y(near))
        c2 = c.start(own, own, c.slots(1), me.at_y(far))
        cs = [c.start(own, own, c.slots(1), sibling)]
        fill(1)
        c1.wait_recv()
        passed = block(near)
        c3 = c.start(passed, passed, c.slots(1), me.at_y(far))
        cs.append(c.start(passed, passed, c.slots(1), sibling))
        c2.wait_recv()
        cs.append(c.start(block(far), block(far), c.slots(1), sibling))
        c3.wait_recv()
        cs.append(c.start(block(me.y2), block(me.y2), c.slots(1), sibling))
        for copy in cs:
            copy.wait_recv()


def both(ref, cols):
    return jnp.concatenate([ref[h, ..., cols].reshape(256, -1) for h in (0, 1)], axis=0)


def main_kernel(
    rows_ref, obs, b0, b1, noise, root_prior, region_prior, root_out, region_low,
    xa, xb, xc, w0, w1, *rest,
):
    sets, rest = [rest[9 * i:9 * i + 9] for i in range(3)], rest[27:]
    fa, fb, slab, rx, own, full, inv_a, inv_d, x0, send_sems, recv_sems = rest
    sa, sb, sc = [refs[8] for refs in sets]
    me = Place()
    copies = Copies(send_sems, recv_sems)
    barrier = pltpu.get_barrier_semaphore()
    for peer in [me.at_y(me.y1), me.at_y(me.y3)] + [me.at_z(d) for d in range(1, 8)] + [
        me.at_r(lax.rem(me.r + d, 8)) for d in range(1, 8)
    ]:
        pl.semaphore_signal(barrier, inc=1, device_id=peer, device_id_type=MESH)

    count = rows_ref[0]
    lane = lax.broadcasted_iota(jnp.int32, (1, 128), 1)
    for g in range(8):
        wrow = jnp.where(lane + 128 * g < count, noise[g:g + 1, :], 0.0)
        wt = jnp.broadcast_to(wrow, (128, 128)).T
        for q in range(4):
            rows, cols = slice(128 * g, 128 * g + 128), slice(128 * q, 128 * q + 128)
            w1[rows, cols] = (b1[rows, cols].astype(F32) * wt).astype(BF16)
            w0[rows, cols] = (b0[rows, cols].astype(F32) * wt).astype(BF16)

    def dot(a, b):
        return lax.dot_general(a, b, (TN, ((), ())), preferred_element_type=F32)

    def put(ref, h, cols, value):
        ref[h, :, :, cols] = value.reshape(4, 64, value.shape[1])

    def reduction(x, refs):
        half = x.shape[3] // 2
        y_side, z_side, out = refs[:4], refs[4:8], refs[8]
        return Both(
            Reduce(me, copies, x, slice(0, half), True, y_side[0], y_side[1], y_side[2], None, out),
            Reduce(me, copies, x, slice(half, 2 * half), False, z_side[0], z_side[1], z_side[2], z_side[3], out),
        )

    def gathering(part, whole):
        half = whole.shape[3] // 2
        return Both(
            Gather(me, copies, part, whole, slice(0, half), False),
            Gather(me, copies, part, whole, slice(half, 2 * half), True),
        )

    halves = [(0, slice(0, 256)), (1, slice(256, 512))]
    for h, half in halves:
        put(xa, h, slice(0, 512), 0.5 * (dot(w1[:, half], b1[...]) + dot(b1[:, half], w1[...])))
    pl.semaphore_wait(barrier, 16)
    red_a, red_b, red_c = [reduction(x, refs) for x, refs in zip((xa, xb, xc), sets)]
    gat_a, gat_b = gathering(sa, fa), gathering(sb, fb)
    red_a(0)
    for h, half in halves:
        put(xb, h, slice(0, 512), dot(w0[:, half], b1[...]))
        put(xb, h, slice(512, 768), dot(w1[:, half], obs[...]))
    red_a(1)
    red_b(0)
    for h, half in halves:
        put(xc, h, slice(0, 512), 0.5 * (dot(w0[:, half], b0[...]) + dot(b0[:, half], w0[...])))
        put(xc, h, slice(512, 768), dot(w0[:, half], obs[...]))
    for step in (red_a, 2), (red_a, 3), (red_b, 1), (red_a, 4), (red_a, 5), (red_b, 2), (red_a, 6), (gat_a, 0), \
            (red_b, 3), (gat_a, 1), (gat_a, 2), (red_b, 4), (gat_a, 3), (red_c, 0), (gat_a, 4), (red_b, 5), \
            (gat_a, 5), (red_b, 6), (gat_b, 0), (gat_a, 6):
        step[0](step[1])
    for h, half in halves:
        inv_a[half, :] = region_prior[half, :] + fa[h].reshape(256, 512)
    tasks = {
        4: (red_c, 1), 8: (gat_b, 1), 12: (red_c, 2), 17: (gat_b, 2), 21: (red_c, 3), 26: (gat_b, 3),
        30: (red_c, 4), 36: (gat_b, 4), 41: (red_c, 5), 48: (gat_b, 5), 56: (red_c, 6),
    }

    def serve(point):
        if point in tasks:
            tasks[point][0](tasks[point][1])

    spd_inverse(inv_a, inv_d, serve=serve)
    P3 = split(-inv_a[...])
    u = dot3(split(sb[...].reshape(16, 768)[:, :512]), P3, MM)
    u3 = split(u)
    gat_b(6)
    a01 = split(both(fb, slice(0, 512)))
    w13 = split(both(fb, slice(512, 768)))
    s = sc[...].reshape(16, 768)[:, :512] - dot3(u3, a01, NT)
    t = sc[...].reshape(16, 768)[:, 512:] - dot3(u3, w13, MM)
    slab[:, :, :512] = s.reshape(2, 8, 512)
    slab[:, :, 512:] = t.reshape(2, 8, 256)
    root = RootSum(me, copies, slab, rx, own, full)

    def fill(part):
        if part == 0:
            x0[:, :512] = dot3(P3, a01, NT)
        else:
            x0[:, 512:] = dot3(P3, w13, MM)

    root.run(fill)
    for h in (0, 1):
        half = slice(256 * h, 256 * h + 256)
        inv_a[half, :] = root_prior[half, :] + full[h, :, :512]
    spd_inverse(inv_a, inv_d)
    mean = dot3(split(-inv_a[...]), split(both(full, slice(512, 768))), MM)
    root_out[...] = mean
    region_low[...] = (x0[:, 512:] - dot3(split(x0[:, :512]), split(mean), MM)).astype(BF16)
    copies.finish()


def estimate(observations, basis_root, basis_region, noise_weights, leaf_rows, root_prior, region_prior):
    vm = lambda *shape: pltpu.VMEM(shape, F32)

    def reduce_set(w):
        v = w // 2
        return [vm(2, 2, 64, v), vm(2, 64, v), vm(8, 2, 8, v), vm(8, 128),
                vm(2, 2, 8, v), vm(2, 8, v), vm(8, 2, 4, 8, v), vm(2, 4, 8, v), vm(2, 8, w)]

    spec = pl.BlockSpec(memory_space=pltpu.VMEM)
    return pl.pallas_call(
        main_kernel,
        out_shape=(jax.ShapeDtypeStruct((512, 256), F32), jax.ShapeDtypeStruct((512, 256), BF16)),
        in_specs=[pl.BlockSpec(memory_space=pltpu.SMEM)] + [spec] * 6,
        out_specs=(spec, spec),
        scratch_shapes=[vm(2, 4, 64, 512), vm(2, 4, 64, 768), vm(2, 4, 64, 768),
                        pltpu.VMEM((1024, 512), BF16), pltpu.VMEM((1024, 512), BF16)]
        + reduce_set(512) + reduce_set(768) + reduce_set(768) + [vm(2, 4, 64, 512), vm(2, 4, 64, 768)]
        + [vm(2, 8, 768), vm(8, 8, 768), vm(8, 768), vm(2, 256, 768)]
        + [vm(512, 512), vm(128, 128), vm(512, 768)]
        + [pltpu.SemaphoreType.DMA((168,)), pltpu.SemaphoreType.DMA((168,))],
        compiler_params=pltpu.CompilerParams(collective_id=0, has_side_effects=True, vmem_limit_bytes=60 << 20),
    )(leaf_rows, observations, basis_root, basis_region, noise_weights.reshape(8, 128), root_prior, region_prior[0])


def body(
    observations, basis_root, basis_region, noise_weights, leaf_rows, root_prior, region_prior
):
    root_mean, region_low = estimate(
        observations, basis_root, basis_region, noise_weights, leaf_rows, root_prior, region_prior
    )
    fitted = jnp.dot(basis_root, root_mean.astype(jnp.bfloat16), preferred_element_type=jnp.float32)
    fitted = fitted + jnp.dot(basis_region, region_low, preferred_element_type=jnp.float32)
    return (fitted, root_mean)


def solution(mesh):
    placed = (
        P(("region", "sub"), None),
        P(("region", "sub"), None),
        P(("region", "sub"), None),
        P(("region", "sub")),
        P(("region", "sub")),
        P(),
        P("region", None, None),
    )
    return jax.shard_map(
        body,
        mesh=mesh,
        in_specs=placed,
        out_specs=(P(("region", "sub"), None), P()),
        check_vma=False,
    )
```

```python
import functools

import jax
import jax.numpy as jnp
from jax import lax
from jax.experimental import pallas as pl
from jax.experimental.pallas import tpu as pltpu
from jax.sharding import PartitionSpec as P

MESH = pl.DeviceIdType.MESH
F32 = jnp.float32
BF16 = jnp.bfloat16
HI = lax.Precision.HIGHEST

def split(x):
    hi = x.astype(BF16)
    return hi, (x - hi.astype(F32)).astype(BF16)

def dot3(a, b, dims):
    ah, al = a
    bh, bl = b
    d = lambda u, v: lax.dot_general(u, v, (dims, ((), ())), preferred_element_type=F32)
    return d(ah, bh) + (d(ah, bl) + d(al, bh))

MM = ((1,), (0,))

def inv_small(s):
    s = dict(s)
    g = lambda i, j: s[(i, j)] if i >= j else s[(j, i)]
    for k in range(0, 8, 2):
        a, b, c = g(k, k), g(k + 1, k), g(k + 1, k + 1)
        r = 1.0 / (a * c - b * b)
        d00, d01, d11 = c * r, -b * r, a * r
        others = [i for i in range(8) if i not in (k, k + 1)]
        t = {}
        for i in others:
            u, v = g(i, k), g(i, k + 1)
            t[i] = (u * d00 + v * d01, u * d01 + v * d11)
        new = {}
        for i in others:
            for j in others:
                if i >= j:
                    new[(i, j)] = g(i, j) - (t[i][0] * g(j, k) + t[i][1] * g(j, k + 1))
        for i in others:
            for q in (0, 1):
                key = (max(i, k + q), min(i, k + q))
                new[key] = t[i][q]
        new[(k, k)], new[(k + 1, k)], new[(k + 1, k + 1)] = -d00, -d01, -d11
        s = new
    return {key: -v for key, v in s.items()}

def inv128(rows, tmp, serve=None, base=0):
    lane = lax.broadcasted_iota(jnp.int32, (8, 128), 1)
    sub = lax.broadcasted_iota(jnp.int32, (8, 128), 0)
    a = list(rows)
    for p in range(16):
        if serve is not None:
            serve(base + p)
        R = a[p]
        k0 = 8 * p
        inK = (lane >= k0) & (lane < k0 + 8)
        cols = [jnp.broadcast_to(R[:, k0 + j:k0 + j + 1], (8, 128)) for j in range(8)]
        for j in range(8):
            tmp[8 * j:8 * j + 8, :] = cols[j]
        s = {(i, j): tmp[pl.ds(8 * j + i, 8, stride=0), :] for i in range(8) for j in range(i + 1)}
        Rm = jnp.where(inK, jnp.where(lane - k0 == sub, -1.0, 0.0), R)
        tmp[64:72, :] = Rm
        Rb = [tmp[pl.ds(64 + q, 8, stride=0), :] for q in range(8)]
        D = inv_small(s)
        g = lambda i, j: D[(i, j)] if i >= j else D[(j, i)]
        G = []
        for i in range(8):
            t = [g(i, q) * Rb[q] for q in range(8)]
            while len(t) > 1:
                t = [t[m] + t[m + 1] for m in range(0, len(t), 2)]
            G.append(t[0])
        new = G[7]
        for q in range(7):
            new = jnp.where(sub == q, G[q], new)
        Rh, Gh = R.astype(BF16).astype(F32), new.astype(BF16).astype(F32)
        Rl, Gl = R - Rh, new - Gh
        left = jnp.concatenate([Rh, Rh, Rl, Rl], axis=0).astype(BF16)
        right = jnp.concatenate([Gh, Gl, Gh, Gl], axis=0).astype(BF16)
        if p < 15:
            i = p + 1
            c = [jnp.broadcast_to(a[i][:, k0 + j:k0 + j + 1], (8, 128)) * G[j] for j in range(8)]
            while len(c) > 1:
                c = [c[m] + c[m + 1] for m in range(0, len(c), 2)]
            a[i] = jnp.where(inK, 0.0, a[i]) - c[0]
        U = lax.dot_general(left, right, (((0,), (0,)), ((), ())), preferred_element_type=F32)
        for i in range(16):
            if i != p and i != p + 1:
                a[i] = jnp.where(inK, 0.0, a[i]) - U[8 * i:8 * i + 8, :]
        a[p] = new
    return a

def spd_inverse(A, Dbuf, n=512, serve=None):
    nb = n // 128
    def step(k, carry):
        o = k * 128 if serve is not None else pl.multiple_of(k * 128, 128)
        rows = [A[pl.ds(o + 8 * i if serve is not None else pl.multiple_of(o + 8 * i, 8), 8), pl.ds(o, 128)] for i in range(16)]
        out = inv128(rows, Dbuf, serve, 16 * k)
        for i in range(16):
            Dbuf[8 * i:8 * i + 8, :] = -out[i]
        D = split(Dbuf[...])
        Rk = split(A[pl.ds(o, 128), :])
        Ck = split(A[:, pl.ds(o, 128)])
        G = dot3(D, Rk, MM)
        T = dot3(Ck, D, MM)
        U = dot3(Ck, split(G), MM)
        A[...] = A[...] - U
        A[pl.ds(o, 128), :] = G
        A[:, pl.ds(o, 128)] = T
        A[pl.ds(o, 128), pl.ds(o, 128)] = -Dbuf[...]
        return carry
    if serve is None:
        lax.fori_loop(0, nb, step, 0)
    else:
        for k in range(nb):
            step(k, 0)


NT = ((1,), (1,))
TN = ((0,), (0,))


class Copies:
    def __init__(self, send_sems, recv_sems):
        self.send_sems, self.recv_sems, self.used, self.sent = send_sems, recv_sems, 0, []

    def slots(self, count):
        first = self.used
        self.used += count
        return first

    def start(self, source, target, slot, peer):
        copy = pltpu.make_async_remote_copy(
            src_ref=source, dst_ref=target, send_sem=self.send_sems.at[slot], recv_sem=self.recv_sems.at[slot],
            device_id=peer, device_id_type=MESH,
        )
        copy.start()
        self.sent.append(copy)
        return copy

    def finish(self):
        for copy in self.sent:
            copy.wait_send()
        self.sent = []


class Place:
    def __init__(self):
        self.r = lax.axis_index("region")
        s = lax.axis_index("sub")
        self.y, self.z = lax.rem(s, 4), s // 4
        self.core = lax.rem(self.r, 2)
        self.y1 = self.y + 1 - 2 * lax.rem(self.y, 2)
        self.y3 = 3 - self.y
        self.y2 = lax.rem(self.y + 2, 4)

    def at_y(self, y):
        return {"region": self.r, "sub": self.z * 4 + y}

    def at_z(self, d):
        return {"region": self.r, "sub": lax.rem(self.z + d, 8) * 4 + self.y}

    def at_r(self, r):
        return {"region": r, "sub": self.z * 4 + self.y}


class Ring:
    def rows(self, d):
        return pl.ds(pl.multiple_of(lax.rem(self.me.z + d + 8, 8) * 8, 8), 8)

    def up_or_down(self, side):
        return self.me.at_z(1 if side == 0 else 7)


class Reduce(Ring):
    def __init__(self, me, copies, x, cols, y_first, r1, r2, zbuf, part, out):
        self.me, self.copies, self.x, self.cols, self.y_first = me, copies, x, cols, y_first
        self.r1, self.r2, self.zbuf, self.part, self.out = r1, r2, zbuf, part, out
        self.first, self.second = [me.y1, me.y3], [me.y3, me.y1]
        self.c1, self.c2, self.cz = {}, {}, [[], []]
        ring = [self.z_start, lambda: self.z_pass(1), lambda: self.z_pass(2), lambda: self.z_pass(3)]
        if y_first:
            self.steps = [self.y_start, self.y_middle, lambda: (self.y_end(), ring[0]())] + ring[1:] + [self.z_end]
        else:
            self.steps = ring + [lambda: (self.z_end(), self.y_start()), self.y_middle, self.y_end]

    def block(self, h, b):
        return self.x.at[h, b, :, self.cols] if self.y_first else self.part.at[h, b]

    def y_start(self):
        me, c = self.me, self.copies
        for slot in (1, 0):
            for h in (0, 1):
                b = self.first[h] if slot == 0 else me.y2
                self.c1[h, slot] = c.start(self.block(h, b), self.r1.at[h, slot], c.slots(1), me.at_y(self.first[h]))

    def y_middle(self):
        me, c = self.me, self.copies
        for h in (0, 1):
            self.c1[h, 1].wait_recv()
            self.r1[h, 1] = self.r1[h, 1] + self.block(h, self.second[h])[...]
            self.c2[h] = c.start(self.r1.at[h, 1], self.r2.at[h], c.slots(1), me.at_y(self.second[h]))

    def y_end(self):
        for h in (0, 1):
            self.c1[h, 0].wait_recv()
            self.c2[h].wait_recv()
            total = self.r1[h, 0] + self.block(h, self.me.y)[...] + self.r2[h]
            if self.y_first:
                self.r1[h, 0] = total
            else:
                self.out[h, :, self.cols] = total

    def chunk(self, d):
        return self.r1.at[:, 0, self.rows(d), :] if self.y_first else self.x.at[:, :, self.rows(d), self.cols]

    def z_send(self, step):
        c = self.copies
        for side, way in ((0, 1), (1, -1)):
            source, target = self.chunk(way * (4 - step)), self.zbuf.at[4 * side + step]
            if step == 0:
                source, target = source.at[side], target.at[side]
            self.cz[side].append(c.start(source, target, c.slots(1), self.up_or_down(side)))

    def z_start(self):
        self.z_send(0)

    def z_pass(self, step):
        for side, way in ((0, 1), (1, -1)):
            self.cz[side][step - 1].wait_recv()
            part, slot = self.chunk(way * (4 - step)), 4 * side + step - 1
            if step == 1:
                part[side] = part[side] + self.zbuf[slot, side]
            else:
                part[...] = part[...] + self.zbuf[slot]
        self.z_send(step)

    def z_end(self):
        for side in (0, 1):
            self.cz[side][3].wait_recv()
        total = self.chunk(0)[...] + self.zbuf[3] + self.zbuf[7]
        if self.y_first:
            self.out[:, :, self.cols] = total
        else:
            self.part[...] = total


class Gather(Ring):
    def __init__(self, me, copies, slab, full, cols, y_first):
        self.me, self.copies, self.slab, self.full, self.cols, self.y_first = me, copies, slab, full, cols, y_first
        self.c1, self.c2, self.cz = [], [], [[], []]
        ring = [lambda: self.z_send(0), lambda: self.z_pass(1), lambda: self.z_pass(2), lambda: self.z_pass(3)]
        if y_first:
            self.steps = [lambda: (self.place(), self.y_start()), self.y_pass, lambda: (self.y_end(), ring[0]())]
            self.steps += ring[1:] + [self.z_end]
        else:
            self.steps = [lambda: (self.place(), ring[0]())] + ring[1:]
            self.steps += [lambda: (self.z_end(), self.y_start()), self.y_pass, self.y_end]

    def place(self):
        self.full[:, self.me.y, self.rows(0), self.cols] = self.slab[:, :, self.cols]

    def block(self, h, b):
        return self.full.at[h, b, self.rows(0), self.cols] if self.y_first else self.full.at[h, b, :, self.cols]

    def chunk(self, d):
        if self.y_first:
            return self.full.at[:, :, self.rows(d), self.cols]
        return self.full.at[:, self.me.y, self.rows(d), self.cols]

    def y_start(self):
        me, c = self.me, self.copies
        for h, near, far in ((0, me.y3, me.y1), (1, me.y1, me.y3)):
            own = self.block(h, me.y)
            self.c1.append(c.start(own, own, c.slots(1), me.at_y(near)))
            self.c2.append(c.start(own, own, c.slots(1), me.at_y(far)))

    def y_pass(self):
        me, c = self.me, self.copies
        for h, near, far in ((0, me.y3, me.y1), (1, me.y1, me.y3)):
            self.c1[h].wait_recv()
            passed = self.block(h, near)
            self.c2.append(c.start(passed, passed, c.slots(1), me.at_y(far)))

    def y_end(self):
        for copy in self.c2:
            copy.wait_recv()

    def z_send(self, step):
        c = self.copies
        for side, way in ((0, -1), (1, 1)):
            piece = self.chunk(way * step)
            if step == 3:
                piece = piece.at[side]
            self.cz[side].append(c.start(piece, piece, c.slots(1), self.up_or_down(side)))

    def z_pass(self, step):
        for side in (0, 1):
            self.cz[side][step - 1].wait_recv()
        self.z_send(step)

    def z_end(self):
        for side in (0, 1):
            self.cz[side][3].wait_recv()


class Both:
    def __init__(self, *halves):
        self.halves = halves

    def __call__(self, step):
        for half in self.halves:
            half.steps[step]()


class RootSum:
    def __init__(self, me, copies, slab, rx, own, full):
        self.me, self.copies, self.slab, self.rx, self.own, self.full = me, copies, slab, rx, own, full

    def run(self, fill):
        me, c = self.me, self.copies
        slot = c.slots(8)
        for d in range(1, 8):
            peer = lax.rem(me.r + d, 8)
            copy = pltpu.make_async_remote_copy(
                src_ref=self.slab.at[lax.rem(peer, 2)], dst_ref=self.rx.at[me.r],
                send_sem=c.send_sems.at[slot + d - 1], recv_sem=c.recv_sems.at[slot + me.r],
                device_id=me.at_r(peer), device_id_type=MESH,
            )
            copy.start()
            c.sent.append(copy)
        self.rx[me.r] = self.slab[me.core]
        for d in range(1, 8):
            peer = lax.rem(me.r + d, 8)
            pltpu.make_async_remote_copy(
                src_ref=self.slab.at[0], dst_ref=self.rx.at[peer],
                send_sem=c.send_sems.at[slot + d - 1], recv_sem=c.recv_sems.at[slot + peer],
                device_id=me.at_r(peer), device_id_type=MESH,
            ).wait_recv()
        total = self.rx[0]
        for i in range(1, 8):
            total = total + self.rx[i]
        self.own[...] = total
        row = pl.multiple_of(me.y * 64 + me.z * 8, 8)
        self.full[me.core, pl.ds(row, 8), :] = total
        piece = self.full.at[me.core, pl.ds(row, 8), :]
        cz = [c.start(self.own, piece, c.slots(1), me.at_z(d)) for d in (4, 3, 5, 2, 6, 1, 7)]
        fill(0)
        for copy in cz:
            copy.wait_recv()
        near = me.y3 + me.core * (me.y1 - me.y3)
        far = me.y1 + me.core * (me.y3 - me.y1)
        sibling = me.at_r(me.r + 1 - 2 * me.core)

        def block(b):
            return self.full.at[me.core, pl.ds(pl.multiple_of(b * 64, 64), 64), :]

        own = block(me.y)
        c1 = c.start(own, own, c.slots(1), me.at_y(near))
        c2 = c.start(own, own, c.slots(1), me.at_y(far))
        cs = [c.start(own, own, c.slots(1), sibling)]
        fill(1)
        c1.wait_recv()
        passed = block(near)
        c3 = c.start(passed, passed, c.slots(1), me.at_y(far))
        cs.append(c.start(passed, passed, c.slots(1), sibling))
        c2.wait_recv()
        cs.append(c.start(block(far), block(far), c.slots(1), sibling))
        c3.wait_recv()
        cs.append(c.start(block(me.y2), block(me.y2), c.slots(1), sibling))
        for copy in cs:
            copy.wait_recv()


def both(ref, cols):
    return jnp.concatenate([ref[h, ..., cols].reshape(256, -1) for h in (0, 1)], axis=0)


def main_kernel(
    rows_ref, obs_in, b0_in, b1, noise, root_prior_in, region_prior_in, root_out, region_low,
    xa, xb, xc, w0, w1, obs, b0, root_prior, region_prior, load_sems, *rest,
):
    sets, rest = [rest[9 * i:9 * i + 9] for i in range(3)], rest[27:]
    fa, fb, slab, rx, own, full, inv_a, inv_d, x0, send_sems, recv_sems = rest
    sa, sb, sc = [refs[8] for refs in sets]
    loads = [
        pltpu.make_async_copy(source, target, load_sems.at[i])
        for i, (source, target) in enumerate(
            [(b0_in, b0), (obs_in, obs), (region_prior_in, region_prior), (root_prior_in, root_prior)]
        )
    ]
    for load in loads:
        load.start()
    me = Place()
    copies = Copies(send_sems, recv_sems)
    barrier = pltpu.get_barrier_semaphore()
    for peer in [me.at_y(me.y1), me.at_y(me.y3)] + [me.at_z(d) for d in range(1, 8)] + [
        me.at_r(lax.rem(me.r + d, 8)) for d in range(1, 8)
    ]:
        pl.semaphore_signal(barrier, inc=1, device_id=peer, device_id_type=MESH)

    count = rows_ref[0]
    lane = lax.broadcasted_iota(jnp.int32, (1, 128), 1)
    def weigh(source, target):
        for g in range(8):
            wrow = jnp.where(lane + 128 * g < count, noise[g:g + 1, :], 0.0)
            wt = jnp.broadcast_to(wrow, (128, 128)).T
            for q in range(4):
                rows, cols = slice(128 * g, 128 * g + 128), slice(128 * q, 128 * q + 128)
                target[rows, cols] = (source[rows, cols].astype(F32) * wt).astype(BF16)

    weigh(b1, w1)

    def dot(a, b):
        return lax.dot_general(a, b, (TN, ((), ())), preferred_element_type=F32)

    def put(ref, h, cols, value):
        ref[h, :, :, cols] = value.reshape(4, 64, value.shape[1])

    def reduction(x, refs):
        half = x.shape[3] // 2
        y_side, z_side, out = refs[:4], refs[4:8], refs[8]
        return Both(
            Reduce(me, copies, x, slice(0, half), True, y_side[0], y_side[1], y_side[2], None, out),
            Reduce(me, copies, x, slice(half, 2 * half), False, z_side[0], z_side[1], z_side[2], z_side[3], out),
        )

    def gathering(part, whole):
        half = whole.shape[3] // 2
        return Both(
            Gather(me, copies, part, whole, slice(0, half), False),
            Gather(me, copies, part, whole, slice(half, 2 * half), True),
        )

    halves = [(0, slice(0, 256)), (1, slice(256, 512))]
    for h, half in halves:
        put(xa, h, slice(0, 512), 0.5 * (dot(w1[:, half], b1[...]) + dot(b1[:, half], w1[...])))
    pl.semaphore_wait(barrier, 16)
    red_a, red_b, red_c = [reduction(x, refs) for x, refs in zip((xa, xb, xc), sets)]
    gat_a, gat_b = gathering(sa, fa), gathering(sb, fb)
    red_a(0)
    loads[0].wait()
    loads[1].wait()
    weigh(b0, w0)
    for h, half in halves:
        put(xb, h, slice(0, 512), dot(w0[:, half], b1[...]))
        put(xb, h, slice(512, 768), dot(w1[:, half], obs[...]))
    red_a(1)
    red_b(0)
    for h, half in halves:
        put(xc, h, slice(0, 512), 0.5 * (dot(w0[:, half], b0[...]) + dot(b0[:, half], w0[...])))
        put(xc, h, slice(512, 768), dot(w0[:, half], obs[...]))
    for step in (red_a, 2), (red_a, 3), (red_a, 4), (red_b, 1), (red_a, 5), (red_a, 6), (gat_a, 0), (red_b, 2), \
            (gat_a, 1), (red_b, 3), (gat_a, 2), (gat_a, 3), (red_c, 0), (red_b, 4), (gat_a, 4), (red_b, 5), \
            (gat_a, 5), (gat_a, 6):
        step[0](step[1])
    loads[2].wait()
    loads[3].wait()
    for h, half in halves:
        inv_a[half, :] = region_prior[half, :] + fa[h].reshape(256, 512)
    tasks = {
        1: (red_b, 6), 2: (gat_b, 0), 4: (red_c, 1), 9: (gat_b, 1), 13: (red_c, 2), 18: (gat_b, 2), 22: (red_c, 3),
        27: (gat_b, 3), 31: (red_c, 4), 36: (gat_b, 4), 41: (red_c, 5), 47: (gat_b, 5), 56: (red_c, 6),
    }

    def serve(point):
        if point in tasks:
            tasks[point][0](tasks[point][1])

    spd_inverse(inv_a, inv_d, serve=serve)
    P3 = split(-inv_a[...])
    u = dot3(split(sb[...].reshape(16, 768)[:, :512]), P3, MM)
    u3 = split(u)
    gat_b(6)
    a01 = split(both(fb, slice(0, 512)))
    w13 = split(both(fb, slice(512, 768)))
    s = sc[...].reshape(16, 768)[:, :512] - dot3(u3, a01, NT)
    t = sc[...].reshape(16, 768)[:, 512:] - dot3(u3, w13, MM)
    slab[:, :, :512] = s.reshape(2, 8, 512)
    slab[:, :, 512:] = t.reshape(2, 8, 256)
    root = RootSum(me, copies, slab, rx, own, full)

    def fill(part):
        if part == 0:
            x0[:, :512] = dot3(P3, a01, NT)
        else:
            x0[:, 512:] = dot3(P3, w13, MM)

    root.run(fill)
    for h in (0, 1):
        half = slice(256 * h, 256 * h + 256)
        inv_a[half, :] = root_prior[half, :] + full[h, :, :512]
    spd_inverse(inv_a, inv_d)
    mean = dot3(split(-inv_a[...]), split(both(full, slice(512, 768))), MM)
    root_out[...] = mean
    region_low[...] = (x0[:, 512:] - dot3(split(x0[:, :512]), split(mean), MM)).astype(BF16)
    copies.finish()


def estimate(observations, basis_root, basis_region, noise_weights, leaf_rows, root_prior, region_prior):
    vm = lambda *shape: pltpu.VMEM(shape, F32)

    def reduce_set(w):
        v = w // 2
        return [vm(2, 2, 64, v), vm(2, 64, v), vm(8, 2, 8, v), vm(8, 128),
                vm(2, 2, 8, v), vm(2, 8, v), vm(8, 2, 4, 8, v), vm(2, 4, 8, v), vm(2, 8, w)]

    spec = pl.BlockSpec(memory_space=pltpu.VMEM)
    away = pl.BlockSpec(memory_space=pl.ANY)
    return pl.pallas_call(
        main_kernel,
        out_shape=(jax.ShapeDtypeStruct((512, 256), F32), jax.ShapeDtypeStruct((512, 256), BF16)),
        in_specs=[pl.BlockSpec(memory_space=pltpu.SMEM), away, away, spec, spec, away, away],
        out_specs=(spec, spec),
        scratch_shapes=[vm(2, 4, 64, 512), vm(2, 4, 64, 768), vm(2, 4, 64, 768),
                        pltpu.VMEM((1024, 512), BF16), pltpu.VMEM((1024, 512), BF16),
                        pltpu.VMEM((1024, 256), BF16), pltpu.VMEM((1024, 512), BF16), vm(512, 512), vm(512, 512),
                        pltpu.SemaphoreType.DMA((4,))]
        + reduce_set(512) + reduce_set(768) + reduce_set(768) + [vm(2, 4, 64, 512), vm(2, 4, 64, 768)]
        + [vm(2, 8, 768), vm(8, 8, 768), vm(8, 768), vm(2, 256, 768)]
        + [vm(512, 512), vm(128, 128), vm(512, 768)]
        + [pltpu.SemaphoreType.DMA((168,)), pltpu.SemaphoreType.DMA((168,))],
        compiler_params=pltpu.CompilerParams(collective_id=0, has_side_effects=True, vmem_limit_bytes=60 << 20),
    )(leaf_rows, observations, basis_root, basis_region, noise_weights.reshape(8, 128), root_prior, region_prior[0])


def body(
    observations, basis_root, basis_region, noise_weights, leaf_rows, root_prior, region_prior
):
    root_mean, region_low = estimate(
        observations, basis_root, basis_region, noise_weights, leaf_rows, root_prior, region_prior
    )
    fitted = jnp.dot(basis_root, root_mean.astype(jnp.bfloat16), preferred_element_type=jnp.float32)
    fitted = fitted + jnp.dot(basis_region, region_low, preferred_element_type=jnp.float32)
    return (fitted, root_mean)


def solution(mesh):
    placed = (
        P(("region", "sub"), None),
        P(("region", "sub"), None),
        P(("region", "sub"), None),
        P(("region", "sub")),
        P(("region", "sub")),
        P(),
        P("region", None, None),
    )
    return jax.shard_map(
        body,
        mesh=mesh,
        in_specs=placed,
        out_specs=(P(("region", "sub"), None), P()),
        check_vma=False,
    )
```
